32 devices in a mesh: blk: 16 (over z, y, x), rep: 2 (over core).
Axes of the slice: x: 2, y: 2, z: 4, core: 2. Of those that a mesh axis runs over, the one named last changes fastest.
Arguments:
- features: bfloat16 [16384, 128], P(('blk', 'rep')), may hold values from -6 to 6
- cotangent: bfloat16 [16384, 256], P(('blk', 'rep')), may hold values from -0.046875 to 0.046875
- self_weight: float32 [16384], P('blk'), may hold values from 0.2 to 1
- w_first: bfloat16 [128, 256], replicated, may hold values from -0.5 to 0.5
- b_first: float32 [256], replicated, may hold values from -4 to 4
- w_second: bfloat16 [256, 256], replicated, may hold values from -0.375 to 0.375
- block_row: int32 [16, 16, 12], P('blk', 'rep'), may hold values from 0 to 127, as said below
- block_col: int32 [16, 16, 12], P('blk', 'rep'), may hold values from 0 to 127, as said below
- block_slot: int32 [16, 16, 12], P('blk', 'rep'), may hold values from 0 to 11, as said below
- block_count: int32 [16, 16], P('blk', 'rep'), may hold values from 0 to 12, as said below
- block_values: bfloat16 [16, 16, 12, 128, 128], P('blk', 'rep'), as said below
Outputs:
- grad_w1: float32 [128, 256], replicated
- grad_b1: float32 [256], replicated
- grad_w2: float32 [256, 256], replicated
The draws below stay inside these ranges and needn't reach their ends.
Inputs may be any that keep to these rules, and one draw needn't show every extreme that they name: `block_row`: entry k of partition p at distance d names a row block of partition p, from p * 8 to p * 8 + 7; entries with k >= block_count[p, d] are ignored. `block_col`: entry k of partition p at distance d names a column block of partition (p - d) mod 16; no block appears twice among counted entries; block (a, b) is counted if and only if block (b, a) is. `block_slot`: for each partition and distance the 12 slots form a permutation of 0 to 11. `block_count`: some partitions fill all 12 slots at some distance in every draw. `block_values`: the values of block (a, b) are the transpose of those of block (b, a); a block on the diagonal is symmetric.
All inputs are finite; a program needn't handle non-finite values.
Results may differ from the reference program's by a relative error of at most 0.00068.
Values may be sent and summed in bfloat16 or wider, within the bound.
No kernel may reach another device: no remote copies, remote signals or barrier semaphores. Data moves between devices by JAX's collectives and lax.ppermute only.
A program may use at most 64 MiB of HBM per device.

```python
import math
import jax
import jax.numpy as jnp
from jax import lax

F_IN = 128
HID = 256
BS = 128
MOST = 12
NP = 1024
PARTS_SIZE = 16
NODES = 16384
NBLOCKS = 128


def block_plan(key):
    base_key = jax.random.fold_in(key, 4111)
    count_key = jax.random.fold_in(base_key, 1)
    cell_key = jax.random.fold_in(base_key, 2)
    slot_key = jax.random.fold_in(base_key, 3)
    row_blocks = NP // BS
    cells_all = row_blocks * row_blocks
    part_ids = jnp.arange(PARTS_SIZE, dtype=jnp.int32)
    source = part_ids[:, None]
    distance = part_ids[None, :]
    cycle_gap = jnp.minimum(distance, PARTS_SIZE - distance)
    capacity = MOST // (1 + cycle_gap // 4)
    raw_bits = jax.random.randint(count_key, (PARTS_SIZE, PARTS_SIZE), 0, 1 << 20, dtype=jnp.int32)
    diag_count = 1 + raw_bits % min(row_blocks, MOST)
    count_table = jnp.where(cycle_gap <= 1, MOST, raw_bits % (capacity + 1))
    count_table = jnp.where(distance == 0, diag_count, count_table)
    canonical = (distance == 0) | (distance >= 1) & (2 * distance < PARTS_SIZE) | (2 * distance == PARTS_SIZE) & (2 * source < PARTS_SIZE)
    partner = (source - distance) % PARTS_SIZE
    canon_part = jnp.where(canonical, source, partner)
    canon_dist = jnp.where(canonical, distance, (PARTS_SIZE - distance) % PARTS_SIZE)
    canon_part = jnp.broadcast_to(canon_part, (PARTS_SIZE, PARTS_SIZE))
    canon_dist = jnp.broadcast_to(canon_dist, (PARTS_SIZE, PARTS_SIZE))
    counts = count_table[canon_part, canon_dist]
    scores = jax.random.randint(cell_key, (PARTS_SIZE, PARTS_SIZE, cells_all), 0, 1 << 20, dtype=jnp.int32) * cells_all + jnp.arange(cells_all, dtype=jnp.int32)
    cell_order = jnp.argsort(scores, axis=-1, stable=True)[:, :, :MOST].astype(jnp.int32)
    cell_pick = cell_order[canon_part, canon_dist]
    first_idx = cell_pick // row_blocks
    second = cell_pick % row_blocks
    diag_start = raw_bits // 7 % row_blocks
    diag_rows = (diag_start[:, :, None] + jnp.arange(MOST, dtype=jnp.int32)) % row_blocks
    source_three = jnp.broadcast_to(source, (PARTS_SIZE, PARTS_SIZE))[:, :, None]
    partner_three = jnp.broadcast_to(partner, (PARTS_SIZE, PARTS_SIZE))[:, :, None]
    canon_three = jnp.broadcast_to(canonical, (PARTS_SIZE, PARTS_SIZE))[:, :, None]
    zero_three = jnp.broadcast_to(distance == 0, (PARTS_SIZE, PARTS_SIZE))[:, :, None]
    row_ids = jnp.where(zero_three, source_three * row_blocks + diag_rows, jnp.where(canon_three, source_three * row_blocks + first_idx, source_three * row_blocks + second))
    col_ids = jnp.where(zero_three, source_three * row_blocks + diag_rows, jnp.where(canon_three, partner_three * row_blocks + second, partner_three * row_blocks + first_idx))
    slot_scores = jax.random.randint(slot_key, (PARTS_SIZE, PARTS_SIZE, MOST), 0, 1 << 20, dtype=jnp.int32) * MOST + jnp.arange(MOST, dtype=jnp.int32)
    slot_perm = jnp.argsort(slot_scores, axis=-1, stable=True).astype(jnp.int32)
    return (row_ids.astype(jnp.int32), col_ids.astype(jnp.int32), slot_perm, counts.astype(jnp.int32), jnp.broadcast_to(canonical, (PARTS_SIZE, PARTS_SIZE)))


def draw_block_row(key, part):
    return block_plan(key)[0]


def draw_block_col(key, part):
    return block_plan(key)[1]


def draw_block_slot(key, part):
    return block_plan(key)[2]


def draw_block_count(key, part):
    return block_plan(key)[3]


def draw_block_values(key, part):
    row_ids, col_ids, slot_perm, counts, canonical = block_plan(key)
    value_key = jax.random.fold_in(key, 4127)
    value_scale = 0.8 * (BS * (1 + 10 * MOST // (NP // BS))) ** (-0.5)
    first_ident = jnp.where(canonical[:, :, None], row_ids, col_ids)
    second_ident = jnp.where(canonical[:, :, None], col_ids, row_ids)
    block_ident = first_ident * NBLOCKS + second_ident
    inverse = jnp.argsort(slot_perm, axis=-1, stable=True).astype(jnp.int32)
    ident_at_slot = jnp.take_along_axis(block_ident, inverse, axis=-1)
    diag_flag = (jnp.arange(PARTS_SIZE, dtype=jnp.int32) == 0)[:, None, None, None]

    def one_part(part_index):
        idents = ident_at_slot[part_index].reshape(-1)
        drawn_blocks = jax.vmap(lambda ident_now: jax.random.uniform(jax.random.fold_in(value_key, ident_now), (BS, BS), jnp.float32, 0.0, 2.0))(idents)
        drawn_blocks = drawn_blocks.reshape(PARTS_SIZE, MOST, BS, BS)
        turned = jnp.swapaxes(drawn_blocks, 2, 3)
        keep_order = canonical[part_index][:, None, None, None]
        blocks = jnp.where(diag_flag, (drawn_blocks + turned) * 0.5, jnp.where(keep_order, drawn_blocks, turned))
        return (blocks * value_scale).astype(jnp.bfloat16)
    return lax.map(one_part, jnp.arange(PARTS_SIZE, dtype=jnp.int32))


def levels(stream_key, shape, shards, least, largest):
    level = 1.0
    for dim, parts in shards:
        draws = jax.random.uniform(jax.random.fold_in(jax.random.fold_in(stream_key, 6), dim), (parts,), jnp.float32, least / len(shards), largest / len(shards))
        level = level * jnp.repeat(jnp.exp(draws), shape[dim] // parts).reshape((-1,) + (1,) * (len(shape) - 1 - dim))
    return level


def noise(key, extent, scale, bound, split=(), kind=jnp.bfloat16):
    level = levels(key, extent, split, -0.22, 0.18) if split else 1.0
    result = jax.random.normal(key, extent, jnp.float32) * scale * level
    return jnp.minimum(jnp.maximum(result, -bound), bound).astype(kind)


def setup_inputs(seed: int = 0) -> dict:
    key_of = jax.random.split(jax.random.key(seed), 12)
    features = noise(key_of[0], (NODES, F_IN), 1.0, 6.0, ((0, 32),))
    cotangent = noise(key_of[1], (NODES, HID), NODES ** -0.5, 0.046875, ((0, 32),))
    self_weight = jnp.clip(jnp.exp(math.log(1.0) - 1.609438 * jax.random.uniform(key_of[2], (NODES,), jnp.float32) ** levels(key_of[2], (NODES,), ((0, 16),), -0.2, 0.2)), 0.2, 1.0)
    w_first = noise(key_of[3], (F_IN, HID), F_IN ** -0.5, 0.5)
    b_first = noise(key_of[4], (HID,), 1.0, 4.0, (), jnp.float32)
    w_second = noise(key_of[5], (HID, HID), HID ** -0.5, 0.375)
    block_row = draw_block_row(jax.random.fold_in(key_of[11], 71), 0)
    block_col = draw_block_col(jax.random.fold_in(key_of[11], 71), 0)
    block_slot = draw_block_slot(jax.random.fold_in(key_of[11], 71), 0)
    block_count = draw_block_count(jax.random.fold_in(key_of[11], 71), 0)
    block_values = draw_block_values(jax.random.fold_in(key_of[11], 71), 0)
    return {"features": features, "cotangent": cotangent, "self_weight": self_weight, "w_first": w_first, "b_first": b_first, "w_second": w_second, "block_row": block_row, "block_col": block_col, "block_slot": block_slot, "block_count": block_count, "block_values": block_values}


def aggregate(node_feats, self_weight, block_row, block_col, block_slot, block_count, block_values):
    feat_width = node_feats.shape[1]
    row_blocks = NP // BS
    panels = node_feats.reshape(NBLOCKS, BS, feat_width)
    block_range = jnp.arange(MOST, dtype=jnp.int32)
    row_range = jnp.arange(row_blocks, dtype=jnp.int32)

    def one_part(part_entry):
        part_rows, part_cols, part_slots, part_counts, part_values = part_entry

        def one_distance(running, dist_entry):
            row_ids, col_ids, slot_ids, count_now, values_now = dist_entry
            blocks = jnp.take(values_now, slot_ids, axis=0).astype(jnp.float32)
            picked = jnp.take(panels, col_ids, axis=0).astype(jnp.float32)
            product = jnp.einsum("mab,mbf->maf", blocks, picked, precision=lax.Precision.HIGHEST)
            match = ((row_ids % row_blocks)[None, :] == row_range[:, None]) & (block_range < count_now)[None, :]
            onehot = jnp.where(match, 1.0, 0.0).astype(jnp.float32)
            running = running + jnp.einsum("rm,maf->raf", onehot, product, precision=lax.Precision.HIGHEST)
            return running, None

        start_sum = jnp.zeros((row_blocks, BS, feat_width), jnp.float32)
        running, _ = lax.scan(one_distance, start_sum, (part_rows, part_cols, part_slots, part_counts, part_values))
        return running

    part_sums = lax.map(one_part, (block_row, block_col, block_slot, block_count, block_values))
    return part_sums.reshape(NODES, feat_width) + self_weight[:, None] * node_feats.astype(jnp.float32)


def reference(features, cotangent, self_weight, w_first, b_first, w_second, block_row, block_col, block_slot, block_count, block_values):
    aggregated = aggregate(features, self_weight, block_row, block_col, block_slot, block_count, block_values).astype(jnp.bfloat16)
    pre_act = jnp.dot(aggregated, w_first, preferred_element_type=jnp.float32) + b_first
    hidden = jax.nn.silu(pre_act).astype(jnp.bfloat16)
    back_agg = aggregate(cotangent, self_weight, block_row, block_col, block_slot, block_count, block_values).astype(jnp.bfloat16)
    grad_w2 = jnp.dot(hidden.T, back_agg, preferred_element_type=jnp.float32)
    squashed = jax.nn.sigmoid(pre_act)
    d_hidden = jnp.dot(back_agg, w_second.T, preferred_element_type=jnp.float32)
    grad_pre = (d_hidden * squashed * (1.0 + pre_act * (1.0 - squashed))).astype(jnp.bfloat16)
    grad_w1 = jnp.dot(aggregated.T, grad_pre, preferred_element_type=jnp.float32)
    grad_b1 = jnp.sum(grad_pre.astype(jnp.float32), axis=0)
    return (grad_w1, grad_b1, grad_w2)
```

```python
import functools

import jax
import jax.numpy as jnp
from jax import lax
from jax.experimental import pallas as pl
from jax.experimental.pallas import tpu as pltpu
from jax.sharding import PartitionSpec as P


def passed_along(value, axis, steps):
    count = lax.axis_size(axis)
    pairs = [(source, (source + steps) % count) for source in range(count)]
    return lax.ppermute(value, axis, pairs)


def contribute(running, panel_now, position, tables):
    local_rows, local_cols, live_mask, ordered = tables
    row_ids = lax.dynamic_index_in_dim(local_rows, position, 0, keepdims=False)
    col_ids = lax.dynamic_index_in_dim(local_cols, position, 0, keepdims=False)
    live_now = lax.dynamic_index_in_dim(live_mask, position, 0, keepdims=False)
    blocks = lax.dynamic_index_in_dim(ordered, position, 0, keepdims=False)
    picked = jnp.take(panel_now, col_ids, axis=0)
    product = jnp.einsum("mab,mbf->maf", blocks, picked, preferred_element_type=jnp.float32)
    row_range = jnp.arange(panel_now.shape[0], dtype=jnp.int32)
    onehot = jnp.where(row_ids[None, :] == row_range[:, None], live_now[None, :], 0.0)
    return running + jnp.einsum("rm,maf->raf", onehot, product, precision=lax.Precision.HIGHEST)


def walk_shards(
    features,
    cotangent,
    self_weight,
    w_first,
    b_first,
    w_second,
    block_row,
    block_col,
    block_slot,
    block_count,
    block_values,
):
    rep_index = lax.axis_index("rep")
    bit_count = lax.axis_size("rep").bit_length() - 1
    cycle_steps = block_values.shape[1]
    most_blocks = block_values.shape[2]
    block_size = block_values.shape[3]
    in_width = features.shape[1]
    hid_width = cotangent.shape[1]
    x_full, g_full = (
        lax.all_gather(features, "rep", axis=0, tiled=True),
        lax.all_gather(cotangent, "rep", axis=0, tiled=True),
    )
    rows_total = x_full.shape[0]
    row_blocks = rows_total // block_size
    live_mask = jnp.where(
        jnp.arange(most_blocks, dtype=jnp.int32)[None, :] < block_count[0][:, None], 1.0, 0.0
    ).astype(jnp.float32)
    ordered = jnp.take_along_axis(block_values[0], block_slot[0][:, :, None, None], axis=1)
    tables = (block_row[0] % row_blocks, block_col[0] % row_blocks, live_mask, ordered)
    x_panel = x_full.reshape(row_blocks, block_size, in_width)
    g_panel = g_full.reshape(row_blocks, block_size, hid_width)
    moving_x = x_panel
    for bit_level in range(bit_count):
        shifted_x = passed_along(moving_x, "blk", cycle_steps << bit_level)
        moving_x = jnp.where(rep_index >> bit_level & 1 == 1, shifted_x, moving_x)
    first_x = contribute(
        jnp.zeros((row_blocks, block_size, in_width), jnp.float32), moving_x, 0, tables
    )

    def walk_x(position, loop_state):
        held_panel, running = loop_state
        held_panel = passed_along(held_panel, "blk", 1)
        return (held_panel, contribute(running, held_panel, position, tables))

    total_x = lax.fori_loop(1, cycle_steps, walk_x, (moving_x, first_x))[1]
    moving_g = g_panel
    for bit_level in range(bit_count):
        shifted_g = passed_along(moving_g, "blk", cycle_steps << bit_level)
        moving_g = jnp.where(rep_index >> bit_level & 1 == 1, shifted_g, moving_g)
    first_g = contribute(
        jnp.zeros((row_blocks, block_size, hid_width), jnp.float32), moving_g, 0, tables
    )

    def walk_g(position, loop_state):
        held_panel, running = loop_state
        held_panel = passed_along(held_panel, "blk", 1)
        return (held_panel, contribute(running, held_panel, position, tables))

    total_g = lax.fori_loop(1, cycle_steps, walk_g, (moving_g, first_g))[1]
    part_x_all = total_x.reshape(rows_total, in_width)
    part_g_all = total_g.reshape(rows_total, hid_width)
    part_x, part_g = lax.psum((part_x_all, part_g_all), "rep")
    aggregated = (part_x + self_weight[:, None] * x_full.astype(jnp.float32)).astype(jnp.bfloat16)
    pre_act = jnp.dot(aggregated, w_first, preferred_element_type=jnp.float32) + b_first
    hidden = jax.nn.silu(pre_act).astype(jnp.bfloat16)
    back_agg = (part_g + self_weight[:, None] * g_full.astype(jnp.float32)).astype(jnp.bfloat16)
    grad_w2 = jnp.einsum("nh,nk->hk", hidden, back_agg, preferred_element_type=jnp.float32)
    squashed = jax.nn.sigmoid(pre_act)
    d_hidden = jnp.einsum("nk,hk->nh", back_agg, w_second, preferred_element_type=jnp.float32)
    grad_pre = (d_hidden * squashed * (1.0 + pre_act * (1.0 - squashed))).astype(jnp.bfloat16)
    grad_w1 = jnp.einsum("nf,nh->fh", aggregated, grad_pre, preferred_element_type=jnp.float32)
    grad_b1 = jnp.sum(grad_pre.astype(jnp.float32), axis=0)
    grad_w1, grad_b1, grad_w2 = lax.psum((grad_w1, grad_b1, grad_w2), "blk")
    return (grad_w1, grad_b1, grad_w2)

BF16, F32, I32 = jnp.bfloat16, jnp.float32, jnp.int32
LANES = 128
VMEM_SPEC = pl.BlockSpec(memory_space=pltpu.VMEM)
SMEM_SPEC = pl.BlockSpec(memory_space=pltpu.SMEM)
ANY_SPEC = pl.BlockSpec(memory_space=pl.ANY)


def send(value, target):
    pairs = []
    for p in range(16):
        for r in range(2):
            to = target(p, r)
            if to is not None:
                pairs.append((p * 2 + r, to[0] * 2 + to[1]))
    return lax.ppermute(value, ("blk", "rep"), pairs)


def to_sibling(value):
    return send(value, lambda p, r: (p, 1 - r))


def first_way(value):
    return send(value, lambda p, r: (p ^ (1 + r), r))


def second_way(value):
    return send(value, lambda p, r: (p ^ (2 - r), r))


def z_pairs(value):
    return send(value, lambda p, r: (p ^ 4, r))


def z_middle(value):
    return send(value, lambda p, r: (p ^ 12, r) if p // 4 in (1, 2) else None)


def z_outward(value):
    return send(value, lambda p, r: (p ^ 4, r) if p // 4 in (1, 2) else None)


def assemble_kernel(place, feat, cot, got_tile, got_first, panel):
    core = place[1]
    half = feat.shape[0]
    rolled = pltpu.roll(got_first[...].astype(F32), LANES // 2, 1).astype(BF16)
    lane = lax.broadcasted_iota(I32, (half, LANES), 1)
    mine = cot[:, :LANES]

    @pl.when(core == 0)
    def _():
        panel[0:half, :] = feat[...]
        panel[half : 2 * half, :] = got_tile[...]
        panel[2 * half :, :] = jnp.where(lane < LANES // 2, mine, rolled)

    @pl.when(core == 1)
    def _():
        panel[0:half, :] = got_tile[...]
        panel[half : 2 * half, :] = cot[:, LANES:]
        panel[2 * half :, :] = jnp.where(lane < LANES // 2, rolled, mine)


def entry_of(place, kind):
    step_one, step_two, slot = kind
    p, core = place[0], place[1]
    z, w = p >> 2, p & 3
    if step_one:
        w = w ^ (1 + core)
    if step_two:
        w = w ^ (2 - core)
    upper = z >> 1
    z = (z, z ^ 1, 2 - upper, 3 - 3 * upper)[slot]
    d = (p - (z * 4 + w)) & 15
    return (d >> 3) ^ core, d & 7


def gather_kernel(kinds, first, last, place, table, start, own, other, *rest):
    n = len(kinds)
    panels, (out, acc, xbuf, abuf, sems) = rest[:n], rest[n:]
    blocks = acc.shape[1]
    size = acc.shape[2]
    rows = blocks * size
    half = rows // 2
    where = [entry_of(place, kind) for kind in kinds]
    if not first:
        start_copy = pltpu.make_async_copy(start, acc, sems.at[2, 0])
        start_copy.start()
    for j in range(n):
        away, dist = where[j]
        pltpu.make_async_copy(panels[j], xbuf.at[j], sems.at[0, j]).start()

        @pl.when(away == 0)
        def _():
            pltpu.make_async_copy(own.at[dist], abuf.at[j], sems.at[1, j]).start()

        @pl.when(away != 0)
        def _():
            pltpu.make_async_copy(other.at[dist], abuf.at[j], sems.at[1, j]).start()

    if not first:
        start_copy.wait()
    for j in range(n):
        away, dist = where[j]
        base = (away * 8 + dist) * 16
        pltpu.make_async_copy(panels[j], xbuf.at[j], sems.at[0, j]).wait()
        pltpu.make_async_copy(own.at[0], abuf.at[j], sems.at[1, j]).wait()
        if first and j == 0:
            for b in range(blocks):
                weight = start[b * size : (b + 1) * size, :]
                side, at = b // (blocks // 2), b % (blocks // 2)
                acc[0, b] = weight * xbuf[0, b * size : (b + 1) * size, :].astype(F32)
                acc[1 + side, b] = weight * xbuf[0, rows + at * size : rows + (at + 1) * size, :].astype(F32)
                acc[2 - side, b] = jnp.zeros((size, LANES), F32)

        def block(k, carry):
            entry = table[base + k]
            row, col, slot = entry & 7, (entry >> 3) & 7, entry >> 6
            tile = xbuf[j, pl.ds(pl.multiple_of(col * size, size), size), :]
            pack = xbuf[j, pl.ds(pl.multiple_of(rows + (col & 3) * size, size), size), :]
            product = jnp.dot(
                abuf[j, slot], jnp.concatenate([tile, pack], axis=1), preferred_element_type=F32
            )
            acc[0, row] += product[:, :LANES]
            acc[1 + (col >> 2), row] += product[:, LANES:]
            return carry

        lax.fori_loop(0, table[base + 12], block, 0)
    if last:
        core = place[1]
        lane = lax.broadcasted_iota(I32, (size, LANES), 1)
        valid = (lane < LANES // 2) == (core == 0)
        for b in range(blocks):
            out[b * size : (b + 1) * size, :] = acc[0, b].astype(BF16)
            joined = acc[1, b] + pltpu.roll(acc[2, b], LANES // 2, 1)
            turned = pltpu.roll(joined, LANES // 2, 1)
            both = jnp.where(core == 0, joined, turned)
            out[rows + b * size : rows + (b + 1) * size, :] = jnp.where(valid, both, 0.0).astype(BF16)
    else:
        pltpu.make_async_copy(acc, out, sems.at[2, 0]).start()
        pltpu.make_async_copy(acc, out, sems.at[2, 0]).wait()


def gather_call(kinds, first, last, place, table, start, own, other, panels):
    n = len(kinds)
    most, size = own.shape[1], own.shape[2]
    rows = panels[0].shape[0] * 2 // 3
    blocks = rows // size
    acc_shape = (3, blocks, size, LANES)
    out = (
        jax.ShapeDtypeStruct((2 * rows, LANES), BF16) if last else jax.ShapeDtypeStruct(acc_shape, F32)
    )
    return pl.pallas_call(
        functools.partial(gather_kernel, kinds, first, last),
        out_shape=out,
        in_specs=[SMEM_SPEC, SMEM_SPEC, VMEM_SPEC if first else ANY_SPEC] + [ANY_SPEC] * (2 + n),
        out_specs=VMEM_SPEC if last else ANY_SPEC,
        scratch_shapes=[
            pltpu.VMEM(acc_shape, F32),
            pltpu.VMEM((n, panels[0].shape[0], LANES), BF16),
            pltpu.VMEM((n, most, size, size), BF16),
            pltpu.SemaphoreType.DMA((3, n)),
        ],
        compiler_params=pltpu.CompilerParams(vmem_limit_bytes=24 << 20),
        cost_estimate=pl.CostEstimate(
            flops=n * 6 * 2 * size * size * 2 * LANES, bytes_accessed=n * 800000, transcendentals=0
        ),
    )(place, table, start, own, other, *panels)


def dense_kernel(place, mine, theirs, w_one, bias, w_two, out):
    core = place[1]
    rows = mine.shape[0] // 2
    agg = jnp.where(core == 0, mine[:rows, :], theirs[:rows, :])
    upper = jnp.where(core == 0, theirs[:rows, :], mine[:rows, :])
    back = jnp.concatenate([mine[rows:, :] + theirs[rows:, :], upper], axis=1)
    pre = jnp.dot(agg, w_one[...], preferred_element_type=F32) + bias[...]
    squashed = 1.0 / (1.0 + jnp.exp(-pre))
    hidden = (pre * squashed).astype(BF16)
    d_hidden = lax.dot_general(back, w_two[...], (((1,), (1,)), ((), ())), preferred_element_type=F32)
    grad_pre = (d_hidden * squashed * (1.0 + pre * (1.0 - squashed))).astype(BF16)
    over_rows = (((0,), (0,)), ((), ()))
    two = lax.dot_general(hidden, back, over_rows, preferred_element_type=F32)
    one = lax.dot_general(agg, grad_pre, over_rows, preferred_element_type=F32)
    bias_row = jnp.sum(grad_pre.astype(F32), axis=0, keepdims=True)
    quarter = one.shape[0] // 4
    corner = place[0] & 3
    for piece in range(4):
        at = piece ^ corner
        span = slice(piece * quarter, (piece + 1) * quarter)
        out[at, 0:quarter, :] = one[span, :]
        out[at, quarter : 2 * quarter, :] = two[span, :LANES]
        out[at, 2 * quarter : 3 * quarter, :] = two[span, LANES:]
        out[at, 3 * quarter :, :] = jnp.broadcast_to(bias_row, (8, LANES))


def spread_kernel(place, *refs):
    pieces, (one, bias, two) = refs[:8], refs[8:]
    core, corner = place[1], place[0] & 3
    quarter = one.shape[0] // 4
    for k in range(4):
        rows = pl.ds(pl.multiple_of((k ^ corner) * quarter, quarter), quarter)
        below = pl.ds(pl.multiple_of(4 * quarter + (k ^ corner) * quarter, quarter), quarter)
        mine, theirs = pieces[k], pieces[4 + k]
        low = jnp.where(core == 0, mine[...], theirs[...])
        high = jnp.where(core == 0, theirs[...], mine[...])
        one[rows, :LANES] = low[:quarter, :]
        one[rows, LANES:] = high[:quarter, :]
        two[rows, :LANES] = low[quarter : 2 * quarter, :]
        two[rows, LANES:] = low[2 * quarter : 3 * quarter, :]
        two[below, :LANES] = high[quarter : 2 * quarter, :]
        two[below, LANES:] = high[2 * quarter : 3 * quarter, :]
        if k == 0:
            bias[:, :LANES] = low[3 * quarter : 3 * quarter + 1, :]
            bias[:, LANES:] = high[3 * quarter : 3 * quarter + 1, :]


def mesh_shards(
    features,
    cotangent,
    self_weight,
    w_first,
    b_first,
    w_second,
    block_row,
    block_col,
    block_slot,
    block_count,
    block_values,
):
    p, r = lax.axis_index("blk"), lax.axis_index("rep")
    place = jnp.stack([p, r]).astype(I32)
    even = r == 0
    half = features.shape[0]
    rows = 2 * half
    size = block_values.shape[3]
    blocks = rows // size
    hid = w_first.shape[1]

    got_tile = to_sibling(jnp.where(even, cotangent[:, LANES:], features))
    got_first = to_sibling(cotangent[:, :LANES])
    panel = pl.pallas_call(
        assemble_kernel,
        out_shape=jax.ShapeDtypeStruct((3 * half, LANES), BF16),
        in_specs=[SMEM_SPEC] + [VMEM_SPEC] * 4,
        out_specs=VMEM_SPEC,
    )(place, features, cotangent, got_tile, got_first)

    own = block_values[0]
    other = to_sibling(own)
    entries = block_row[0] % blocks + blocks * (block_col[0] % blocks) + blocks * blocks * block_slot[0]
    filler = jnp.zeros((entries.shape[0], 16 - entries.shape[1] - 1), I32)
    own_table = jnp.concatenate([entries, block_count[0][:, None], filler], axis=1)
    table = jnp.concatenate([own_table, to_sibling(own_table)], axis=0).reshape(-1)
    weights = jnp.broadcast_to(self_weight[:, None], (rows, LANES))

    middle = (p // 4 == 1) | (p // 4 == 2)

    def quad(value):
        one = first_way(value)
        return [value, one, second_way(value), second_way(one)]

    slot_a = z_pairs(panel)
    near = z_middle(panel)
    group_o = quad(panel)
    far = z_middle(slot_a)
    group_a = quad(slot_a)
    slot_b = jnp.where(middle, near, z_outward(near))
    group_b = quad(slot_b)
    slot_c = jnp.where(middle, far, z_outward(far))
    group_c = quad(slot_c)
    ways = [(0, 0), (1, 0), (0, 1), (1, 1)]

    def kinds(slot):
        return [way + (slot,) for way in ways]

    acc = gather_call(
        tuple(kinds(0) + kinds(1)), True, False, place, table, weights, own, other, group_o + group_a
    )
    summed = gather_call(
        tuple(kinds(2) + kinds(3)), False, True, place, table, acc, own, other, group_b + group_c
    )
    from_sibling = to_sibling(summed)

    side = hid // 2
    w_one = lax.dynamic_slice_in_dim(w_first, r * side, side, 1)
    bias = lax.dynamic_slice_in_dim(b_first, r * side, side, 0)[None, :]
    w_two = lax.dynamic_slice_in_dim(w_second, r * side, side, 0)
    pieces = pl.pallas_call(
        dense_kernel,
        out_shape=jax.ShapeDtypeStruct((4, 3 * side // 4 + 8, LANES), F32),
        in_specs=[SMEM_SPEC] + [VMEM_SPEC] * 5,
        out_specs=VMEM_SPEC,
    )(place, summed, from_sibling, w_one, bias, w_two)

    def in_plane(value, k):
        return send(value, lambda p, r: (p ^ k, r))

    got = [in_plane(pieces[k], k) for k in (1, 2, 3)]
    total = (pieces[0] + got[0]) + (got[1] + got[2])
    across = [in_plane(total, 4 * k) for k in (1, 2, 3)]
    total = (total + across[0]) + (across[1] + across[2])
    full = [total] + [in_plane(total, k) for k in (1, 2, 3)]
    back = [to_sibling(value) for value in full]
    grad_w1, grad_b1, grad_w2 = pl.pallas_call(
        spread_kernel,
        out_shape=(
            jax.ShapeDtypeStruct((side, hid), F32),
            jax.ShapeDtypeStruct((1, hid), F32),
            jax.ShapeDtypeStruct((hid, hid), F32),
        ),
        in_specs=[SMEM_SPEC] + [VMEM_SPEC] * 8,
        out_specs=(VMEM_SPEC,) * 3,
    )(place, *full, *back)
    return (grad_w1, grad_b1.reshape(hid), grad_w2)


def solution(mesh):
    placed = (
        P(("blk", "rep"), None),
        P(("blk", "rep"), None),
        P("blk"),
        P(),
        P(),
        P(),
        P("blk", "rep", None),
        P("blk", "rep", None),
        P("blk", "rep", None),
        P("blk", "rep"),
        P("blk", "rep", None, None, None),
    )
    fits = mesh.shape["blk"] == 16 and mesh.shape["rep"] == 2
    return jax.shard_map(
        mesh_shards if fits else walk_shards, mesh=mesh, in_specs=placed, out_specs=(P(), P(), P()), check_vma=False
    )
```

```python
import functools

import jax
import jax.numpy as jnp
from jax import lax
from jax.experimental import pallas as pl
from jax.experimental.pallas import tpu as pltpu
from jax.sharding import PartitionSpec as P


def passed_along(value, axis, steps):
    count = lax.axis_size(axis)
    pairs = [(source, (source + steps) % count) for source in range(count)]
    return lax.ppermute(value, axis, pairs)


def contribute(running, panel_now, position, tables):
    local_rows, local_cols, live_mask, ordered = tables
    row_ids = lax.dynamic_index_in_dim(local_rows, position, 0, keepdims=False)
    col_ids = lax.dynamic_index_in_dim(local_cols, position, 0, keepdims=False)
    live_now = lax.dynamic_index_in_dim(live_mask, position, 0, keepdims=False)
    blocks = lax.dynamic_index_in_dim(ordered, position, 0, keepdims=False)
    picked = jnp.take(panel_now, col_ids, axis=0)
    product = jnp.einsum("mab,mbf->maf", blocks, picked, preferred_element_type=jnp.float32)
    row_range = jnp.arange(panel_now.shape[0], dtype=jnp.int32)
    onehot = jnp.where(row_ids[None, :] == row_range[:, None], live_now[None, :], 0.0)
    return running + jnp.einsum("rm,maf->raf", onehot, product, precision=lax.Precision.HIGHEST)


def walk_shards(
    features,
    cotangent,
    self_weight,
    w_first,
    b_first,
    w_second,
    block_row,
    block_col,
    block_slot,
    block_count,
    block_values,
):
    rep_index = lax.axis_index("rep")
    bit_count = lax.axis_size("rep").bit_length() - 1
    cycle_steps = block_values.shape[1]
    most_blocks = block_values.shape[2]
    block_size = block_values.shape[3]
    in_width = features.shape[1]
    hid_width = cotangent.shape[1]
    x_full, g_full = (
        lax.all_gather(features, "rep", axis=0, tiled=True),
        lax.all_gather(cotangent, "rep", axis=0, tiled=True),
    )
    rows_total = x_full.shape[0]
    row_blocks = rows_total // block_size
    live_mask = jnp.where(
        jnp.arange(most_blocks, dtype=jnp.int32)[None, :] < block_count[0][:, None], 1.0, 0.0
    ).astype(jnp.float32)
    ordered = jnp.take_along_axis(block_values[0], block_slot[0][:, :, None, None], axis=1)
    tables = (block_row[0] % row_blocks, block_col[0] % row_blocks, live_mask, ordered)
    x_panel = x_full.reshape(row_blocks, block_size, in_width)
    g_panel = g_full.reshape(row_blocks, block_size, hid_width)
    moving_x = x_panel
    for bit_level in range(bit_count):
        shifted_x = passed_along(moving_x, "blk", cycle_steps << bit_level)
        moving_x = jnp.where(rep_index >> bit_level & 1 == 1, shifted_x, moving_x)
    first_x = contribute(
        jnp.zeros((row_blocks, block_size, in_width), jnp.float32), moving_x, 0, tables
    )

    def walk_x(position, loop_state):
        held_panel, running = loop_state
        held_panel = passed_along(held_panel, "blk", 1)
        return (held_panel, contribute(running, held_panel, position, tables))

    total_x = lax.fori_loop(1, cycle_steps, walk_x, (moving_x, first_x))[1]
    moving_g = g_panel
    for bit_level in range(bit_count):
        shifted_g = passed_along(moving_g, "blk", cycle_steps << bit_level)
        moving_g = jnp.where(rep_index >> bit_level & 1 == 1, shifted_g, moving_g)
    first_g = contribute(
        jnp.zeros((row_blocks, block_size, hid_width), jnp.float32), moving_g, 0, tables
    )

    def walk_g(position, loop_state):
        held_panel, running = loop_state
        held_panel = passed_along(held_panel, "blk", 1)
        return (held_panel, contribute(running, held_panel, position, tables))

    total_g = lax.fori_loop(1, cycle_steps, walk_g, (moving_g, first_g))[1]
    part_x_all = total_x.reshape(rows_total, in_width)
    part_g_all = total_g.reshape(rows_total, hid_width)
    part_x, part_g = lax.psum((part_x_all, part_g_all), "rep")
    aggregated = (part_x + self_weight[:, None] * x_full.astype(jnp.float32)).astype(jnp.bfloat16)
    pre_act = jnp.dot(aggregated, w_first, preferred_element_type=jnp.float32) + b_first
    hidden = jax.nn.silu(pre_act).astype(jnp.bfloat16)
    back_agg = (part_g + self_weight[:, None] * g_full.astype(jnp.float32)).astype(jnp.bfloat16)
    grad_w2 = jnp.einsum("nh,nk->hk", hidden, back_agg, preferred_element_type=jnp.float32)
    squashed = jax.nn.sigmoid(pre_act)
    d_hidden = jnp.einsum("nk,hk->nh", back_agg, w_second, preferred_element_type=jnp.float32)
    grad_pre = (d_hidden * squashed * (1.0 + pre_act * (1.0 - squashed))).astype(jnp.bfloat16)
    grad_w1 = jnp.einsum("nf,nh->fh", aggregated, grad_pre, preferred_element_type=jnp.float32)
    grad_b1 = jnp.sum(grad_pre.astype(jnp.float32), axis=0)
    grad_w1, grad_b1, grad_w2 = lax.psum((grad_w1, grad_b1, grad_w2), "blk")
    return (grad_w1, grad_b1, grad_w2)

BF16, F32, I32 = jnp.bfloat16, jnp.float32, jnp.int32
LANES = 128
VMEM_SPEC = pl.BlockSpec(memory_space=pltpu.VMEM)
SMEM_SPEC = pl.BlockSpec(memory_space=pltpu.SMEM)
HBM_SPEC = pl.BlockSpec(memory_space=pltpu.HBM)


def send(value, target):
    pairs = []
    for p in range(16):
        for r in range(2):
            to = target(p, r)
            if to is not None:
                pairs.append((p * 2 + r, to[0] * 2 + to[1]))
    return lax.ppermute(value, ("blk", "rep"), pairs)


def to_sibling(value):
    return send(value, lambda p, r: (p, 1 - r))


def first_way(value):
    return send(value, lambda p, r: (p ^ (1 + r), r))


def second_way(value):
    return send(value, lambda p, r: (p ^ (2 - r), r))


def z_pairs(value):
    return send(value, lambda p, r: (p ^ 4, r))


def z_middle(value):
    return send(value, lambda p, r: (p ^ 12, r) if p // 4 in (1, 2) else None)


def z_outward(value):
    return send(value, lambda p, r: (p ^ 4, r) if p // 4 in (1, 2) else None)


def pack_kernel(feat, cot, row, col, slot, count, mine, give, table):
    core = lax.axis_index("rep")
    listed = (row[...] & 7) + 8 * (col[...] & 7) + 64 * slot[...]
    dists, most = listed.shape
    table[:dists, :most] = listed
    table[dists : dists + 1, :dists] = count[...]
    half, deep = feat.shape[0], feat.shape[0] // 2
    lane = lax.broadcasted_iota(I32, (deep, LANES), 1)
    above, below = cot[:deep, :LANES], cot[deep:, :LANES]
    above_turned = pltpu.roll(above.astype(F32), LANES // 2, 1).astype(BF16)
    below_turned = pltpu.roll(below.astype(F32), LANES // 2, 1).astype(BF16)
    low = jnp.where(lane < LANES // 2, above, below_turned)
    high = jnp.where(lane < LANES // 2, above_turned, below)

    @pl.when(core == 0)
    def _():
        mine[:half, :] = feat[...]
        mine[half:, :] = low
        give[:half, :] = cot[:, LANES:]
        give[half:, :] = high

    @pl.when(core == 1)
    def _():
        mine[:half, :] = cot[:, LANES:]
        mine[half:, :] = high
        give[:half, :] = feat[...]
        give[half:, :] = low


def entry_of(p, core, kind):
    step_one, step_two, slot = kind
    z, w = p >> 2, p & 3
    if step_one:
        w = w ^ (1 + core)
    if step_two:
        w = w ^ (2 - core)
    upper = z >> 1
    z = (z, z ^ 1, 2 - upper, 3 - 3 * upper)[slot]
    d = (p - (z * 4 + w)) & 15
    return (d >> 3) ^ core, d & 7


UNROLL = 4
FLOPS = 300000000


def gather_kernel(kinds, near, own_table, other_table, start, own, other, *rest):
    n = len(kinds)
    first, last = kinds[0] == (0, 0, 0), kinds[-1] == (1, 1, 3)
    sources, acc, rest = rest[:n], rest[n], rest[n + 1 :]
    if last:
        out, rest = rest[0], rest[1:]
    abuf, table, sems = rest[:3]
    panels = sources if near else [rest[3].at[j] for j in range(n)]
    most = abuf.shape[1]
    blocks = acc.shape[1] - 1
    size = acc.shape[2]
    part = sources[0].shape[0] // 2
    deep = part * 2 // 3
    core = lax.axis_index("rep")
    where = [entry_of(lax.axis_index("blk"), core, kind) for kind in kinds]
    for j in range(n):
        away, dist = where[j]
        if not near:
            pltpu.make_async_copy(sources[j], panels[j], sems.at[1, j]).start()

        @pl.when(away == 0)
        def _():
            pltpu.make_async_copy(own.at[dist], abuf.at[j], sems.at[0, j]).start()

        @pl.when(away != 0)
        def _():
            pltpu.make_async_copy(other.at[dist], abuf.at[j], sems.at[0, j]).start()

    def spot(col):
        side = ((col >> 2) ^ core) * part
        return (
            pl.ds(pl.multiple_of(side + (col & 3) * size, size), size),
            pl.ds(pl.multiple_of(side + deep + (col & 1) * size, size), size),
            (col >> 1) & 1,
        )

    dists = own.shape[0]
    for j in range(n):
        away, dist = where[j]
        for k in range(most):
            table[j, k] = jnp.where(away == 0, own_table[dist, k], other_table[dist, k])
        table[j, most] = jnp.where(away == 0, own_table[dists, dist], other_table[dists, dist])
    for j in range(n):
        count = table[j, most]
        if not near:
            pltpu.make_async_copy(sources[j], panels[j], sems.at[1, j]).wait()
        if first and j == 0:
            for b in range(blocks):
                weight = jnp.transpose(jnp.broadcast_to(start[b : b + 1, :], (size, LANES)))
                tile, pack, _ = spot(b)
                lanes = (b >> 1) & 1
                acc[0, b] = weight * panels[0][tile, :].astype(F32)
                acc[1 + lanes, b] = weight * panels[0][pack, :].astype(F32)
                acc[2 - lanes, b] = jnp.zeros((size, LANES), F32)
        pltpu.make_async_copy(own.at[0], abuf.at[j], sems.at[0, j]).wait()

        def step(g, carry):
            found = []
            for i in range(UNROLL):
                k = g * UNROLL + i
                entry = table[j, jnp.minimum(k, most - 1)]
                tile, pack, lanes = spot((entry >> 3) & 7)
                row = jnp.where(k < count, entry & 7, blocks)
                right = jnp.concatenate([panels[j][tile, :], panels[j][pack, :]], axis=1)
                product = jnp.dot(abuf[j, entry >> 6], right, preferred_element_type=F32)
                found.append((row, lanes, product))
            for row, lanes, product in found:
                acc[0, row] += product[:, :LANES]
                acc[1 + lanes, row] += product[:, LANES:]
            return carry

        lax.fori_loop(0, (count + UNROLL - 1) // UNROLL, step, 0)
    if last:
        rows = blocks * size
        lane = lax.broadcasted_iota(I32, (size, LANES), 1)
        valid = (lane < LANES // 2) == (core == 0)
        for b in range(blocks):
            out[b * size : (b + 1) * size, :] = acc[0, b].astype(BF16)
            joined = acc[1, b] + pltpu.roll(acc[2, b], LANES // 2, 1)
            turned = pltpu.roll(joined, LANES // 2, 1)
            both = jnp.where(core == 0, joined, turned)
            out[rows + b * size : rows + (b + 1) * size, :] = jnp.where(valid, both, 0.0).astype(BF16)


def gather_call(kinds, near, tables, start, own, other, panels):
    n = len(kinds)
    first, last = kinds[0] == (0, 0, 0), kinds[-1] == (1, 1, 3)
    most, size = own.shape[1], own.shape[2]
    rows = panels[0].shape[0] * 2 // 3
    sums = jax.ShapeDtypeStruct((3, rows // size + 1, size, LANES), F32)
    outs = (sums, jax.ShapeDtypeStruct((2 * rows, LANES), BF16)) if last else (sums,)
    return pl.pallas_call(
        functools.partial(gather_kernel, kinds, near),
        out_shape=outs,
        in_specs=[SMEM_SPEC, SMEM_SPEC, VMEM_SPEC, HBM_SPEC, HBM_SPEC]
        + [VMEM_SPEC if near else HBM_SPEC] * n,
        out_specs=(VMEM_SPEC,) * len(outs),
        input_output_aliases={} if first else {2: 0},
        scratch_shapes=[
            pltpu.VMEM((n, most, size, size), BF16),
            pltpu.SMEM((n, most + 1), I32),
            pltpu.SemaphoreType.DMA((2, n)),
        ]
        + ([] if near else [pltpu.VMEM((n,) + panels[0].shape, BF16)]),
        compiler_params=pltpu.CompilerParams(vmem_limit_bytes=16 << 20),
        cost_estimate=pl.CostEstimate(flops=n * FLOPS, bytes_accessed=n * 800000, transcendentals=0),
    )(*tables, start, own, other, *panels)


def dense_kernel(place, mine, theirs, w_first, b_first, w_second, *rest):
    outs, (one, two) = rest[:4], rest[4:]
    core = place[1]
    side = one.shape[1]
    ours = pl.ds(pl.multiple_of(core * side, side), side)
    rows = mine.shape[0] // 2
    agg = jnp.where(core == 0, mine[:rows, :], theirs[:rows, :])
    upper = jnp.where(core == 0, theirs[:rows, :], mine[:rows, :])
    back = jnp.concatenate([mine[rows:, :] + theirs[rows:, :], upper], axis=1)
    pre = jnp.dot(agg, w_first[:, ours], preferred_element_type=F32) + b_first[:, ours]
    squashed = 1.0 / (1.0 + jnp.exp(-pre))
    hidden = (pre * squashed).astype(BF16)
    d_hidden = lax.dot_general(
        back, w_second[ours, :], (((1,), (1,)), ((), ())), preferred_element_type=F32
    )
    grad_pre = (d_hidden * squashed * (1.0 + pre * (1.0 - squashed))).astype(BF16)
    over_rows = (((0,), (0,)), ((), ()))
    two[...] = lax.dot_general(hidden, back, over_rows, preferred_element_type=F32)
    one[...] = lax.dot_general(agg, grad_pre, over_rows, preferred_element_type=F32)
    bias_row = jnp.sum(grad_pre.astype(F32), axis=0, keepdims=True)
    quarter = one.shape[0] // 4
    corner = place[0] & 3
    for k in range(4):
        span = pl.ds(pl.multiple_of((k ^ corner) * quarter, quarter), quarter)
        outs[k][0:quarter, :] = one[span, :]
        outs[k][quarter : 2 * quarter, :] = two[span, :LANES]
        outs[k][2 * quarter : 3 * quarter, :] = two[span, LANES:]
        outs[k][3 * quarter :, :] = jnp.broadcast_to(bias_row, (8, LANES))


def spread_kernel(place, *refs):
    pieces, (one, bias, two) = refs[:8], refs[8:]
    core, corner = place[1], place[0] & 3
    quarter = one.shape[0] // 4
    for k in range(4):
        rows = pl.ds(pl.multiple_of((k ^ corner) * quarter, quarter), quarter)
        below = pl.ds(pl.multiple_of(4 * quarter + (k ^ corner) * quarter, quarter), quarter)
        mine, theirs = pieces[k], pieces[4 + k]
        low = jnp.where(core == 0, mine[...], theirs[...])
        high = jnp.where(core == 0, theirs[...], mine[...])
        one[rows, :LANES] = low[:quarter, :]
        one[rows, LANES:] = high[:quarter, :]
        two[rows, :LANES] = low[quarter : 2 * quarter, :]
        two[rows, LANES:] = low[2 * quarter : 3 * quarter, :]
        two[below, :LANES] = high[quarter : 2 * quarter, :]
        two[below, LANES:] = high[2 * quarter : 3 * quarter, :]
        if k == 0:
            bias[:, :LANES] = low[3 * quarter : 3 * quarter + 1, :]
            bias[:, LANES:] = high[3 * quarter : 3 * quarter + 1, :]


def mesh_shards(
    features,
    cotangent,
    self_weight,
    w_first,
    b_first,
    w_second,
    block_row,
    block_col,
    block_slot,
    block_count,
    block_values,
):
    p, r = lax.axis_index("blk"), lax.axis_index("rep")
    place = jnp.stack([p, r]).astype(I32)
    half = features.shape[0]
    rows = 2 * half
    size = block_values.shape[3]
    blocks = rows // size
    hid = w_first.shape[1]

    mine, give, own_table = pl.pallas_call(
        pack_kernel,
        out_shape=(jax.ShapeDtypeStruct((3 * half // 2, LANES), BF16),) * 2
        + (jax.ShapeDtypeStruct((2 * block_row.shape[1], LANES), I32),),
        in_specs=[VMEM_SPEC] * 6,
        out_specs=(VMEM_SPEC,) * 3,
    )(features, cotangent, block_row[0], block_col[0], block_slot[0], block_count)
    panel = jnp.concatenate([mine, to_sibling(give)], axis=0)

    own = pltpu.with_memory_space_constraint(block_values[0], pltpu.HBM)
    other = pltpu.with_memory_space_constraint(to_sibling(own), pltpu.HBM)
    tables = (own_table, to_sibling(own_table))
    weights = self_weight.reshape(blocks, size)

    middle = (p // 4 == 1) | (p // 4 == 2)

    def named(name, move, value, *after):
        if after:
            value = lax.optimization_barrier((value,) + after)[0]
        with jax.named_scope(name):
            return move(value)

    def products(name, start, work, near=False):
        kinds = tuple(kind for kind, _ in work)
        with jax.named_scope(name):
            return gather_call(kinds, near, tables, start, own, other, [panel for _, panel in work])

    one_o = named("TuO", first_way, panel)
    two_o = named("TvO", second_way, panel)
    slot_a = named("TP1", z_pairs, panel)
    near = named("TP2", z_middle, panel)
    both_o = named("TvuO", second_way, one_o)
    far = named("TP3b", z_middle, slot_a, one_o)
    one_a = named("TuA", first_way, slot_a, two_o)
    slot_b = jnp.where(middle, near, named("TP3a", z_outward, near, one_o))
    two_a = named("TvA", z_pairs, two_o, slot_b)
    (acc,) = products("TK0", weights, [((0, 0, 0), panel), ((1, 0, 0), one_o), ((0, 1, 0), two_o)])
    one_b = named("TuB", first_way, slot_b, both_o, one_a)
    two_b = named("TvB", second_way, slot_b, one_a, acc)
    slot_c = jnp.where(middle, far, named("TP4", z_outward, far))
    both_b = named("TvuB", second_way, one_b)
    (acc,) = products("TK1", acc, [((1, 1, 0), both_o), ((0, 0, 1), slot_a), ((1, 0, 1), one_a), ((0, 0, 2), slot_b)])
    both_a = named("TvuA", z_pairs, both_o, two_a)
    one_c = named("TuC", first_way, slot_c, two_b, acc)
    two_c = named("TvC", second_way, slot_c, both_b)
    (acc,) = products("TK2", acc, [((0, 1, 1), two_a), ((1, 0, 2), one_b), ((0, 1, 2), two_b)])
    both_c = named("TvuC", second_way, one_c, acc)
    (acc,) = products("TK3", acc, [((1, 1, 1), both_a), ((1, 1, 2), both_b), ((0, 0, 3), slot_c), ((1, 0, 3), one_c), ((0, 1, 3), two_c)], True)
    _, summed = products("TK4", acc, [((1, 1, 3), both_c)], True)
    from_sibling = to_sibling(summed)

    side = hid // 2
    pieces = pl.pallas_call(
        dense_kernel,
        out_shape=(jax.ShapeDtypeStruct((3 * side // 4 + 8, LANES), F32),) * 4,
        in_specs=[SMEM_SPEC] + [VMEM_SPEC] * 5,
        out_specs=(VMEM_SPEC,) * 4,
        scratch_shapes=[pltpu.VMEM((side, side), F32), pltpu.VMEM((side, hid), F32)],
    )(place, summed, from_sibling, w_first, b_first[None, :], w_second)

    def in_plane(value, k):
        return send(value, lambda p, r: (p ^ k, r))

    got = [in_plane(pieces[k], k) for k in (1, 2, 3)]
    total = (pieces[0] + got[0]) + (got[1] + got[2])
    across = [in_plane(total, 4 * k) for k in (1, 2, 3)]
    total = (total + across[0]) + (across[1] + across[2])
    full = [total] + [in_plane(total, k) for k in (1, 2, 3)]
    back = [to_sibling(value) for value in full]
    grad_w1, grad_b1, grad_w2 = pl.pallas_call(
        spread_kernel,
        out_shape=(
            jax.ShapeDtypeStruct((side, hid), F32),
            jax.ShapeDtypeStruct((1, hid), F32),
            jax.ShapeDtypeStruct((hid, hid), F32),
        ),
        in_specs=[SMEM_SPEC] + [VMEM_SPEC] * 8,
        out_specs=(VMEM_SPEC,) * 3,
    )(place, *full, *back)
    return (grad_w1, grad_b1.reshape(hid), grad_w2)


def solution(mesh):
    placed = (
        P(("blk", "rep"), None),
        P(("blk", "rep"), None),
        P("blk"),
        P(),
        P(),
        P(),
        P("blk", "rep", None),
        P("blk", "rep", None),
        P("blk", "rep", None),
        P("blk", "rep"),
        P("blk", "rep", None, None, None),
    )
    fits = mesh.shape["blk"] == 16 and mesh.shape["rep"] == 2
    return jax.shard_map(
        mesh_shards if fits else walk_shards, mesh=mesh, in_specs=placed, out_specs=(P(), P(), P()), check_vma=False
    )
```

```python
import functools

import jax
import jax.numpy as jnp
from jax import lax
from jax.experimental import pallas as pl
from jax.experimental.pallas import tpu as pltpu
from jax.sharding import PartitionSpec as P


def passed_along(value, axis, steps):
    count = lax.axis_size(axis)
    pairs = [(source, (source + steps) % count) for source in range(count)]
    return lax.ppermute(value, axis, pairs)


def contribute(running, panel_now, position, tables):
    local_rows, local_cols, live_mask, ordered = tables
    row_ids = lax.dynamic_index_in_dim(local_rows, position, 0, keepdims=False)
    col_ids = lax.dynamic_index_in_dim(local_cols, position, 0, keepdims=False)
    live_now = lax.dynamic_index_in_dim(live_mask, position, 0, keepdims=False)
    blocks = lax.dynamic_index_in_dim(ordered, position, 0, keepdims=False)
    picked = jnp.take(panel_now, col_ids, axis=0)
    product = jnp.einsum("mab,mbf->maf", blocks, picked, preferred_element_type=jnp.float32)
    row_range = jnp.arange(panel_now.shape[0], dtype=jnp.int32)
    onehot = jnp.where(row_ids[None, :] == row_range[:, None], live_now[None, :], 0.0)
    return running + jnp.einsum("rm,maf->raf", onehot, product, precision=lax.Precision.HIGHEST)


def walk_shards(
    features,
    cotangent,
    self_weight,
    w_first,
    b_first,
    w_second,
    block_row,
    block_col,
    block_slot,
    block_count,
    block_values,
):
    rep_index = lax.axis_index("rep")
    bit_count = lax.axis_size("rep").bit_length() - 1
    cycle_steps = block_values.shape[1]
    most_blocks = block_values.shape[2]
    block_size = block_values.shape[3]
    in_width = features.shape[1]
    hid_width = cotangent.shape[1]
    x_full, g_full = (
        lax.all_gather(features, "rep", axis=0, tiled=True),
        lax.all_gather(cotangent, "rep", axis=0, tiled=True),
    )
    rows_total = x_full.shape[0]
    row_blocks = rows_total // block_size
    live_mask = jnp.where(
        jnp.arange(most_blocks, dtype=jnp.int32)[None, :] < block_count[0][:, None], 1.0, 0.0
    ).astype(jnp.float32)
    ordered = jnp.take_along_axis(block_values[0], block_slot[0][:, :, None, None], axis=1)
    tables = (block_row[0] % row_blocks, block_col[0] % row_blocks, live_mask, ordered)
    x_panel = x_full.reshape(row_blocks, block_size, in_width)
    g_panel = g_full.reshape(row_blocks, block_size, hid_width)
    moving_x = x_panel
    for bit_level in range(bit_count):
        shifted_x = passed_along(moving_x, "blk", cycle_steps << bit_level)
        moving_x = jnp.where(rep_index >> bit_level & 1 == 1, shifted_x, moving_x)
    first_x = contribute(
        jnp.zeros((row_blocks, block_size, in_width), jnp.float32), moving_x, 0, tables
    )

    def walk_x(position, loop_state):
        held_panel, running = loop_state
        held_panel = passed_along(held_panel, "blk", 1)
        return (held_panel, contribute(running, held_panel, position, tables))

    total_x = lax.fori_loop(1, cycle_steps, walk_x, (moving_x, first_x))[1]
    moving_g = g_panel
    for bit_level in range(bit_count):
        shifted_g = passed_along(moving_g, "blk", cycle_steps << bit_level)
        moving_g = jnp.where(rep_index >> bit_level & 1 == 1, shifted_g, moving_g)
    first_g = contribute(
        jnp.zeros((row_blocks, block_size, hid_width), jnp.float32), moving_g, 0, tables
    )

    def walk_g(position, loop_state):
        held_panel, running = loop_state
        held_panel = passed_along(held_panel, "blk", 1)
        return (held_panel, contribute(running, held_panel, position, tables))

    total_g = lax.fori_loop(1, cycle_steps, walk_g, (moving_g, first_g))[1]
    part_x_all = total_x.reshape(rows_total, in_width)
    part_g_all = total_g.reshape(rows_total, hid_width)
    part_x, part_g = lax.psum((part_x_all, part_g_all), "rep")
    aggregated = (part_x + self_weight[:, None] * x_full.astype(jnp.float32)).astype(jnp.bfloat16)
    pre_act = jnp.dot(aggregated, w_first, preferred_element_type=jnp.float32) + b_first
    hidden = jax.nn.silu(pre_act).astype(jnp.bfloat16)
    back_agg = (part_g + self_weight[:, None] * g_full.astype(jnp.float32)).astype(jnp.bfloat16)
    grad_w2 = jnp.einsum("nh,nk->hk", hidden, back_agg, preferred_element_type=jnp.float32)
    squashed = jax.nn.sigmoid(pre_act)
    d_hidden = jnp.einsum("nk,hk->nh", back_agg, w_second, preferred_element_type=jnp.float32)
    grad_pre = (d_hidden * squashed * (1.0 + pre_act * (1.0 - squashed))).astype(jnp.bfloat16)
    grad_w1 = jnp.einsum("nf,nh->fh", aggregated, grad_pre, preferred_element_type=jnp.float32)
    grad_b1 = jnp.sum(grad_pre.astype(jnp.float32), axis=0)
    grad_w1, grad_b1, grad_w2 = lax.psum((grad_w1, grad_b1, grad_w2), "blk")
    return (grad_w1, grad_b1, grad_w2)

BF16, F32, I32 = jnp.bfloat16, jnp.float32, jnp.int32
LANES = 128
VMEM_SPEC = pl.BlockSpec(memory_space=pltpu.VMEM)
SMEM_SPEC = pl.BlockSpec(memory_space=pltpu.SMEM)
HBM_SPEC = pl.BlockSpec(memory_space=pltpu.HBM)


def send(value, target):
    pairs = []
    for p in range(16):
        for r in range(2):
            to = target(p, r)
            if to is not None:
                pairs.append((p * 2 + r, to[0] * 2 + to[1]))
    return lax.ppermute(value, ("blk", "rep"), pairs)


def in_hbm(value):
    return pltpu.with_memory_space_constraint(value, pltpu.HBM)


def in_vmem(value):
    return pltpu.with_memory_space_constraint(value, pltpu.VMEM)


def to_sibling(value):
    return send(value, lambda p, r: (p, 1 - r))


def first_way(value):
    return send(value, lambda p, r: (p ^ (1 + r), r))


def second_way(value):
    return send(value, lambda p, r: (p ^ (2 - r), r))


def z_pairs(value):
    return send(value, lambda p, r: (p ^ 4, r))


def z_middle(value):
    return send(value, lambda p, r: (p ^ 12, r) if p // 4 in (1, 2) else None)


def z_outward(value):
    return send(value, lambda p, r: (p ^ 4, r) if p // 4 in (1, 2) else None)


def pack_kernel(away, feat, cot, out):
    core = lax.axis_index("rep")
    core = 1 - core if away else core
    half, deep = feat.shape[0], feat.shape[0] // 2
    lane = lax.broadcasted_iota(I32, (deep, LANES), 1)
    above, below = cot[:deep, :LANES], cot[deep:, :LANES]

    def turned(value):
        return pltpu.roll(value.astype(F32), LANES // 2, 1).astype(BF16)

    @pl.when(core == 0)
    def _():
        out[:half, :] = feat[...]
        out[half : half + deep, :] = jnp.where(lane < LANES // 2, above, turned(below))

    @pl.when(core == 1)
    def _():
        out[:half, :] = cot[:, LANES:]
        out[half : half + deep, :] = jnp.where(lane < LANES // 2, turned(above), below)


def pack_call(away, rows, features, cotangent):
    return pl.pallas_call(
        functools.partial(pack_kernel, away),
        out_shape=pltpu.VMEM((rows, LANES), BF16),
        in_specs=[VMEM_SPEC] * 2,
        out_specs=VMEM_SPEC,
    )(features, cotangent)


def table_kernel(row, col, slot, count, after, table):
    dists, most = row.shape
    table[:dists, :most] = (row[...] & 7) + 8 * (col[...] & 7) + 64 * slot[...]
    table[dists : dists + 1, :dists] = count[...]


def entry_of(p, core, kind):
    step_one, step_two, slot = kind
    z, w = p >> 2, p & 3
    if step_one:
        w = w ^ (1 + core)
    if step_two:
        w = w ^ (2 - core)
    upper = z >> 1
    z = (z, z ^ 1, 2 - upper, 3 - 3 * upper)[slot]
    d = (p - (z * 4 + w)) & 15
    return (d >> 3) ^ core, d & 7


UNROLL = 4
FLOPS = 300000000


def gather_kernel(kinds, near, own_table, other_table, start, own, other, *rest):
    n = len(kinds)
    first, last = kinds[0] == (0, 0, 0), kinds[-1] == (1, 1, 3)
    sources, acc, rest = rest[:n], rest[n], rest[n + 1 :]
    if last:
        out, rest = rest[0], rest[1:]
    abuf, table, sems = rest[:3]
    panels = sources if near else [rest[3].at[j] for j in range(n)]
    most = abuf.shape[1]
    blocks = acc.shape[1] - 1
    size = acc.shape[2]
    part = sources[0].shape[0] // 2
    deep = part * 2 // 3
    core = lax.axis_index("rep")
    where = [entry_of(lax.axis_index("blk"), core, kind) for kind in kinds]
    for j in range(n):
        away, dist = where[j]
        if not near:
            pltpu.make_async_copy(sources[j], panels[j], sems.at[1, j]).start()

        @pl.when(away == 0)
        def _():
            pltpu.make_async_copy(own.at[dist], abuf.at[j], sems.at[0, j]).start()

        @pl.when(away != 0)
        def _():
            pltpu.make_async_copy(other.at[dist], abuf.at[j], sems.at[0, j]).start()

    def spot(col):
        side = ((col >> 2) ^ core) * part
        return (
            pl.ds(pl.multiple_of(side + (col & 3) * size, size), size),
            pl.ds(pl.multiple_of(side + deep + (col & 1) * size, size), size),
            (col >> 1) & 1,
        )

    dists = own.shape[0]
    for j in range(n):
        away, dist = where[j]
        for k in range(most):
            table[j, k] = jnp.where(away == 0, own_table[dist, k], other_table[dist, k])
        table[j, most] = jnp.where(away == 0, own_table[dists, dist], other_table[dists, dist])
    for j in range(n):
        count = table[j, most]
        if not near:
            pltpu.make_async_copy(sources[j], panels[j], sems.at[1, j]).wait()
        if first and j == 0:
            for b in range(blocks):
                weight = jnp.transpose(jnp.broadcast_to(start[b : b + 1, :], (size, LANES)))
                tile, pack, _ = spot(b)
                lanes = (b >> 1) & 1
                acc[0, b] = weight * panels[0][tile, :].astype(F32)
                acc[1 + lanes, b] = weight * panels[0][pack, :].astype(F32)
                acc[2 - lanes, b] = jnp.zeros((size, LANES), F32)
        pltpu.make_async_copy(own.at[0], abuf.at[j], sems.at[0, j]).wait()

        def step(g, carry):
            found = []
            for i in range(UNROLL):
                k = g * UNROLL + i
                entry = table[j, jnp.minimum(k, most - 1)]
                tile, pack, lanes = spot((entry >> 3) & 7)
                row = jnp.where(k < count, entry & 7, blocks)
                right = jnp.concatenate([panels[j][tile, :], panels[j][pack, :]], axis=1)
                product = jnp.dot(abuf[j, entry >> 6], right, preferred_element_type=F32)
                found.append((row, lanes, product))
            for row, lanes, product in found:
                acc[0, row] += product[:, :LANES]
                acc[1 + lanes, row] += product[:, LANES:]
            return carry

        lax.fori_loop(0, (count + UNROLL - 1) // UNROLL, step, 0)
    if last:
        rows = blocks * size
        lane = lax.broadcasted_iota(I32, (size, LANES), 1)
        valid = (lane < LANES // 2) == (core == 0)
        for b in range(blocks):
            out[b * size : (b + 1) * size, :] = acc[0, b].astype(BF16)
            joined = acc[1, b] + pltpu.roll(acc[2, b], LANES // 2, 1)
            turned = pltpu.roll(joined, LANES // 2, 1)
            both = jnp.where(core == 0, joined, turned)
            out[rows + b * size : rows + (b + 1) * size, :] = jnp.where(valid, both, 0.0).astype(BF16)


def gather_call(kinds, near, tables, start, own, other, panels):
    n = len(kinds)
    if near:
        panels = [in_vmem(panel) for panel in panels]
    first, last = kinds[0] == (0, 0, 0), kinds[-1] == (1, 1, 3)
    most, size = own.shape[1], own.shape[2]
    rows = panels[0].shape[0] * 2 // 3
    sums = pltpu.VMEM((3, rows // size + 1, size, LANES), F32)
    outs = (sums, pltpu.VMEM((2 * rows, LANES), BF16)) if last else (sums,)
    start = start if first else in_vmem(start)
    return pl.pallas_call(
        functools.partial(gather_kernel, kinds, near),
        out_shape=outs,
        in_specs=[SMEM_SPEC, SMEM_SPEC, VMEM_SPEC, HBM_SPEC, HBM_SPEC]
        + [VMEM_SPEC if near else HBM_SPEC] * n,
        out_specs=(VMEM_SPEC,) * len(outs),
        input_output_aliases={} if first else {2: 0},
        scratch_shapes=[
            pltpu.VMEM((n, most, size, size), BF16),
            pltpu.SMEM((n, most + 1), I32),
            pltpu.SemaphoreType.DMA((2, n)),
        ]
        + ([] if near else [pltpu.VMEM((n,) + panels[0].shape, BF16)]),
        compiler_params=pltpu.CompilerParams(vmem_limit_bytes=16 << 20),
        cost_estimate=pl.CostEstimate(flops=n * FLOPS, bytes_accessed=n * 800000, transcendentals=0),
    )(*tables, start, own, other, *panels)


def dense_kernel(mine, theirs, w_first, b_first, w_second, *rest):
    outs, (one, two) = rest[:4], rest[4:]
    core = lax.axis_index("rep")
    side = one.shape[1]
    ours = pl.ds(pl.multiple_of(core * side, side), side)
    rows = mine.shape[0] // 2
    agg = jnp.where(core == 0, mine[:rows, :], theirs[:rows, :])
    upper = jnp.where(core == 0, theirs[:rows, :], mine[:rows, :])
    back = jnp.concatenate([mine[rows:, :] + theirs[rows:, :], upper], axis=1)
    pre = jnp.dot(agg, w_first[:, ours], preferred_element_type=F32) + b_first[:, ours]
    squashed = 1.0 / (1.0 + jnp.exp(-pre))
    hidden = (pre * squashed).astype(BF16)
    d_hidden = lax.dot_general(
        back, w_second[ours, :], (((1,), (1,)), ((), ())), preferred_element_type=F32
    )
    grad_pre = (d_hidden * squashed * (1.0 + pre * (1.0 - squashed))).astype(BF16)
    over_rows = (((0,), (0,)), ((), ()))
    two[...] = lax.dot_general(hidden, back, over_rows, preferred_element_type=F32)
    one[...] = lax.dot_general(agg, grad_pre, over_rows, preferred_element_type=F32)
    bias_row = jnp.sum(grad_pre.astype(F32), axis=0, keepdims=True)
    quarter = one.shape[0] // 4
    corner = lax.axis_index("blk") & 3
    for k in range(4):
        span = pl.ds(pl.multiple_of((k ^ corner) * quarter, quarter), quarter)
        outs[k][0:quarter, :] = one[span, :]
        outs[k][quarter : 2 * quarter, :] = two[span, :LANES]
        outs[k][2 * quarter : 3 * quarter, :] = two[span, LANES:]
        outs[k][3 * quarter :, :] = jnp.broadcast_to(bias_row, (8, LANES))


def spread_kernel(*refs):
    pieces, (one, bias, two) = refs[:8], refs[8:]
    core, corner = lax.axis_index("rep"), lax.axis_index("blk") & 3
    quarter = one.shape[0] // 4
    for k in range(4):
        rows = pl.ds(pl.multiple_of((k ^ corner) * quarter, quarter), quarter)
        below = pl.ds(pl.multiple_of(4 * quarter + (k ^ corner) * quarter, quarter), quarter)
        mine, theirs = pieces[k], pieces[4 + k]
        low = jnp.where(core == 0, mine[...], theirs[...])
        high = jnp.where(core == 0, theirs[...], mine[...])
        one[rows, :LANES] = low[:quarter, :]
        one[rows, LANES:] = high[:quarter, :]
        two[rows, :LANES] = low[quarter : 2 * quarter, :]
        two[rows, LANES:] = low[2 * quarter : 3 * quarter, :]
        two[below, :LANES] = high[quarter : 2 * quarter, :]
        two[below, LANES:] = high[2 * quarter : 3 * quarter, :]
        if k == 0:
            bias[:, :LANES] = low[3 * quarter : 3 * quarter + 1, :]
            bias[:, LANES:] = high[3 * quarter : 3 * quarter + 1, :]


def mesh_shards(
    features,
    cotangent,
    self_weight,
    w_first,
    b_first,
    w_second,
    block_row,
    block_col,
    block_slot,
    block_count,
    block_values,
):
    p = lax.axis_index("blk")
    half = features.shape[0]
    rows = 2 * half
    size = block_values.shape[3]
    blocks = rows // size
    hid = w_first.shape[1]

    give = pack_call(True, 3 * half // 2, features, cotangent)
    got = to_sibling(give)
    panel = pack_call(False, 3 * half, features, cotangent)
    panel = lax.dynamic_update_slice(panel, got, (3 * half // 2, 0))

    own = in_hbm(block_values[0])
    held, panel = lax.optimization_barrier((own, panel))
    other = in_hbm(to_sibling(held))
    own_table = pl.pallas_call(
        table_kernel,
        out_shape=jax.ShapeDtypeStruct((2 * block_row.shape[1], LANES), I32),
        in_specs=[VMEM_SPEC] * 4 + [HBM_SPEC],
        out_specs=VMEM_SPEC,
    )(block_row[0], block_col[0], block_slot[0], block_count, panel)
    tables = (own_table, to_sibling(own_table))
    later = lax.optimization_barrier((panel, own_table))[0]
    weights = self_weight.reshape(blocks, size)

    middle = (p // 4 == 1) | (p // 4 == 2)

    def named(name, move, value, *after):
        if after:
            value = lax.optimization_barrier((value,) + after)[0]
        with jax.named_scope(name):
            return move(value)

    def products(name, start, work, near=False):
        kinds = tuple(kind for kind, _ in work)
        with jax.named_scope(name):
            return gather_call(kinds, near, tables, start, own, other, [panel for _, panel in work])

    slot_a = named("TP1", z_pairs, panel)
    one_o = named("TuO", first_way, panel)
    two_o = named("TvO", second_way, panel)
    near = named("TP2", z_middle, later)
    both_o = named("TvuO", second_way, one_o)
    far = named("TP3b", z_middle, slot_a, one_o)
    one_a = named("TuA", first_way, slot_a, two_o)
    slot_b = jnp.where(middle, near, named("TP3a", z_outward, near, slot_a))
    two_a = named("TvA", second_way, slot_a, one_a)
    (first_acc,) = products("TK0", weights, [((0, 0, 0), panel), ((1, 0, 0), one_o), ((0, 1, 0), two_o)])
    one_b = named("TuB", first_way, slot_b, one_a, other)
    two_b = named("TvB", second_way, slot_b, one_a, two_a, first_acc)
    (acc,) = products("TK1", first_acc, [((1, 1, 0), both_o), ((0, 0, 1), slot_a), ((1, 0, 1), one_a), ((1, 0, 2), one_b)])
    slot_c = named("TP4", z_outward, far, both_o, one_a)
    slot_c = jnp.where(middle, lax.optimization_barrier((far, acc))[0], slot_c)
    both_b = named("TvuB", second_way, one_b)
    both_a = named("TvuA", z_pairs, both_o, two_b)
    one_c = named("TuC", first_way, slot_c)
    two_c = named("TvC", second_way, slot_c, two_b)
    (acc,) = products("TK2", acc, [((0, 1, 1), two_a), ((0, 0, 2), slot_b), ((0, 1, 2), two_b)])
    both_c = named("TvuC", second_way, one_c, acc)
    (acc,) = products("TK3", acc, [((1, 1, 1), both_a), ((1, 1, 2), both_b), ((0, 0, 3), slot_c), ((1, 0, 3), one_c), ((0, 1, 3), two_c)], True)
    _, summed = products("TK4", acc, [((1, 1, 3), both_c)], True)
    from_sibling = in_vmem(to_sibling(summed))

    side = hid // 2
    pieces = pl.pallas_call(
        dense_kernel,
        out_shape=(pltpu.VMEM((3 * side // 4 + 8, LANES), F32),) * 4,
        in_specs=[VMEM_SPEC] * 5,
        out_specs=(VMEM_SPEC,) * 4,
        scratch_shapes=[pltpu.VMEM((side, side), F32), pltpu.VMEM((side, hid), F32)],
    )(in_vmem(summed), from_sibling, w_first, b_first[None, :], w_second)

    def in_plane(value, k):
        return send(value, lambda p, r: (p ^ k, r))

    got = [in_plane(pieces[k], k) for k in (1, 2, 3)]
    total = (pieces[0] + got[0]) + (got[1] + got[2])
    across = [in_plane(total, 4 * k) for k in (1, 2, 3)]
    total = (total + across[0]) + (across[1] + across[2])
    full = [total] + [in_plane(total, k) for k in (1, 2, 3)]
    back = [in_vmem(to_sibling(value)) for value in full]
    full = [in_vmem(value) for value in full]
    grad_w1, grad_b1, grad_w2 = pl.pallas_call(
        spread_kernel,
        out_shape=(
            jax.ShapeDtypeStruct((side, hid), F32),
            jax.ShapeDtypeStruct((1, hid), F32),
            jax.ShapeDtypeStruct((hid, hid), F32),
        ),
        in_specs=[VMEM_SPEC] * 8,
        out_specs=(VMEM_SPEC,) * 3,
    )(*full, *back)
    return (grad_w1, grad_b1.reshape(hid), grad_w2)


def solution(mesh):
    placed = (
        P(("blk", "rep"), None),
        P(("blk", "rep"), None),
        P("blk"),
        P(),
        P(),
        P(),
        P("blk", "rep", None),
        P("blk", "rep", None),
        P("blk", "rep", None),
        P("blk", "rep"),
        P("blk", "rep", None, None, None),
    )
    fits = mesh.shape["blk"] == 16 and mesh.shape["rep"] == 2
    return jax.shard_map(
        mesh_shards if fits else walk_shards, mesh=mesh, in_specs=placed, out_specs=(P(), P(), P()), check_vma=False
    )
```

```python
import functools

import jax
import jax.numpy as jnp
from jax import lax
from jax.experimental import pallas as pl
from jax.experimental.pallas import tpu as pltpu
from jax.sharding import PartitionSpec as P


def passed_along(value, axis, steps):
    count = lax.axis_size(axis)
    pairs = [(source, (source + steps) % count) for source in range(count)]
    return lax.ppermute(value, axis, pairs)


def contribute(running, panel_now, position, tables):
    local_rows, local_cols, live_mask, ordered = tables
    row_ids = lax.dynamic_index_in_dim(local_rows, position, 0, keepdims=False)
    col_ids = lax.dynamic_index_in_dim(local_cols, position, 0, keepdims=False)
    live_now = lax.dynamic_index_in_dim(live_mask, position, 0, keepdims=False)
    blocks = lax.dynamic_index_in_dim(ordered, position, 0, keepdims=False)
    picked = jnp.take(panel_now, col_ids, axis=0)
    product = jnp.einsum("mab,mbf->maf", blocks, picked, preferred_element_type=jnp.float32)
    row_range = jnp.arange(panel_now.shape[0], dtype=jnp.int32)
    onehot = jnp.where(row_ids[None, :] == row_range[:, None], live_now[None, :], 0.0)
    return running + jnp.einsum("rm,maf->raf", onehot, product, precision=lax.Precision.HIGHEST)


def walk_shards(
    features,
    cotangent,
    self_weight,
    w_first,
    b_first,
    w_second,
    block_row,
    block_col,
    block_slot,
    block_count,
    block_values,
):
    rep_index = lax.axis_index("rep")
    bit_count = lax.axis_size("rep").bit_length() - 1
    cycle_steps = block_values.shape[1]
    most_blocks = block_values.shape[2]
    block_size = block_values.shape[3]
    in_width = features.shape[1]
    hid_width = cotangent.shape[1]
    x_full, g_full = (
        lax.all_gather(features, "rep", axis=0, tiled=True),
        lax.all_gather(cotangent, "rep", axis=0, tiled=True),
    )
    rows_total = x_full.shape[0]
    row_blocks = rows_total // block_size
    live_mask = jnp.where(
        jnp.arange(most_blocks, dtype=jnp.int32)[None, :] < block_count[0][:, None], 1.0, 0.0
    ).astype(jnp.float32)
    ordered = jnp.take_along_axis(block_values[0], block_slot[0][:, :, None, None], axis=1)
    tables = (block_row[0] % row_blocks, block_col[0] % row_blocks, live_mask, ordered)
    x_panel = x_full.reshape(row_blocks, block_size, in_width)
    g_panel = g_full.reshape(row_blocks, block_size, hid_width)
    moving_x = x_panel
    for bit_level in range(bit_count):
        shifted_x = passed_along(moving_x, "blk", cycle_steps << bit_level)
        moving_x = jnp.where(rep_index >> bit_level & 1 == 1, shifted_x, moving_x)
    first_x = contribute(
        jnp.zeros((row_blocks, block_size, in_width), jnp.float32), moving_x, 0, tables
    )

    def walk_x(position, loop_state):
        held_panel, running = loop_state
        held_panel = passed_along(held_panel, "blk", 1)
        return (held_panel, contribute(running, held_panel, position, tables))

    total_x = lax.fori_loop(1, cycle_steps, walk_x, (moving_x, first_x))[1]
    moving_g = g_panel
    for bit_level in range(bit_count):
        shifted_g = passed_along(moving_g, "blk", cycle_steps << bit_level)
        moving_g = jnp.where(rep_index >> bit_level & 1 == 1, shifted_g, moving_g)
    first_g = contribute(
        jnp.zeros((row_blocks, block_size, hid_width), jnp.float32), moving_g, 0, tables
    )

    def walk_g(position, loop_state):
        held_panel, running = loop_state
        held_panel = passed_along(held_panel, "blk", 1)
        return (held_panel, contribute(running, held_panel, position, tables))

    total_g = lax.fori_loop(1, cycle_steps, walk_g, (moving_g, first_g))[1]
    part_x_all = total_x.reshape(rows_total, in_width)
    part_g_all = total_g.reshape(rows_total, hid_width)
    part_x, part_g = lax.psum((part_x_all, part_g_all), "rep")
    aggregated = (part_x + self_weight[:, None] * x_full.astype(jnp.float32)).astype(jnp.bfloat16)
    pre_act = jnp.dot(aggregated, w_first, preferred_element_type=jnp.float32) + b_first
    hidden = jax.nn.silu(pre_act).astype(jnp.bfloat16)
    back_agg = (part_g + self_weight[:, None] * g_full.astype(jnp.float32)).astype(jnp.bfloat16)
    grad_w2 = jnp.einsum("nh,nk->hk", hidden, back_agg, preferred_element_type=jnp.float32)
    squashed = jax.nn.sigmoid(pre_act)
    d_hidden = jnp.einsum("nk,hk->nh", back_agg, w_second, preferred_element_type=jnp.float32)
    grad_pre = (d_hidden * squashed * (1.0 + pre_act * (1.0 - squashed))).astype(jnp.bfloat16)
    grad_w1 = jnp.einsum("nf,nh->fh", aggregated, grad_pre, preferred_element_type=jnp.float32)
    grad_b1 = jnp.sum(grad_pre.astype(jnp.float32), axis=0)
    grad_w1, grad_b1, grad_w2 = lax.psum((grad_w1, grad_b1, grad_w2), "blk")
    return (grad_w1, grad_b1, grad_w2)

BF16, F32, I32 = jnp.bfloat16, jnp.float32, jnp.int32
LANES = 128
VMEM_SPEC = pl.BlockSpec(memory_space=pltpu.VMEM)
SMEM_SPEC = pl.BlockSpec(memory_space=pltpu.SMEM)
HBM_SPEC = pl.BlockSpec(memory_space=pltpu.HBM)


def send(value, target):
    pairs = []
    for p in range(16):
        for r in range(2):
            to = target(p, r)
            if to is not None:
                pairs.append((p * 2 + r, to[0] * 2 + to[1]))
    return lax.ppermute(value, ("blk", "rep"), pairs)


def in_hbm(value):
    return pltpu.with_memory_space_constraint(value, pltpu.HBM)


def in_vmem(value):
    return pltpu.with_memory_space_constraint(value, pltpu.VMEM)


def to_sibling(value):
    return send(value, lambda p, r: (p, 1 - r))


def first_way(value):
    return send(value, lambda p, r: (p ^ (1 + r), r))


def second_way(value):
    return send(value, lambda p, r: (p ^ (2 - r), r))


def z_pairs(value):
    return send(value, lambda p, r: (p ^ 4, r))


def z_middle(value):
    return send(value, lambda p, r: (p ^ 12, r) if p // 4 in (1, 2) else None)


def z_outward(value):
    return send(value, lambda p, r: (p ^ 4, r) if p // 4 in (1, 2) else None)


def pack_kernel(away, feat, cot, out):
    core = lax.axis_index("rep")
    core = 1 - core if away else core
    half, deep = feat.shape[0], feat.shape[0] // 2
    lane = lax.broadcasted_iota(I32, (deep, LANES), 1)
    above, below = cot[:deep, :LANES], cot[deep:, :LANES]

    def turned(value):
        return pltpu.roll(value.astype(F32), LANES // 2, 1).astype(BF16)

    @pl.when(core == 0)
    def _():
        out[:half, :] = feat[...]
        out[half : half + deep, :] = jnp.where(lane < LANES // 2, above, turned(below))

    @pl.when(core == 1)
    def _():
        out[:half, :] = cot[:, LANES:]
        out[half : half + deep, :] = jnp.where(lane < LANES // 2, turned(above), below)


def pack_call(away, rows, features, cotangent):
    return pl.pallas_call(
        functools.partial(pack_kernel, away),
        out_shape=pltpu.VMEM((rows, LANES), BF16),
        in_specs=[VMEM_SPEC] * 2,
        out_specs=VMEM_SPEC,
    )(features, cotangent)


def table_kernel(row, col, slot, count, after, table):
    dists, most = row.shape
    table[:dists, :most] = (row[...] & 7) + 8 * (col[...] & 7) + 64 * slot[...]
    table[dists : dists + 1, :dists] = count[...]


def entry_of(p, core, kind):
    step_one, step_two, slot = kind
    z, w = p >> 2, p & 3
    if step_one:
        w = w ^ (1 + core)
    if step_two:
        w = w ^ (2 - core)
    upper = z >> 1
    z = (z, z ^ 1, 2 - upper, 3 - 3 * upper)[slot]
    d = (p - (z * 4 + w)) & 15
    return (d >> 3) ^ core, d & 7


UNROLL = 6
FLOPS = 300000000


def gather_kernel(kinds, near, own_table, other_table, start, own, other, *rest):
    n = len(kinds)
    first, last = kinds[0] == (0, 0, 0), kinds[-1] == (1, 1, 3)
    sources, acc, rest = rest[:n], rest[n], rest[n + 1 :]
    if last:
        out, rest = rest[0], rest[1:]
    abuf, table, sems = rest[:3]
    panels = sources if near else [rest[3].at[j] for j in range(n)]
    most = abuf.shape[1]
    blocks = acc.shape[1] - 1
    size = acc.shape[2]
    part = sources[0].shape[0] // 2
    deep = part * 2 // 3
    core = lax.axis_index("rep")
    where = [entry_of(lax.axis_index("blk"), core, kind) for kind in kinds]
    for j in range(n):
        away, dist = where[j]
        if not near:
            pltpu.make_async_copy(sources[j], panels[j], sems.at[1, j]).start()

        @pl.when(away == 0)
        def _():
            pltpu.make_async_copy(own.at[dist], abuf.at[j], sems.at[0, j]).start()

        @pl.when(away != 0)
        def _():
            pltpu.make_async_copy(other.at[dist], abuf.at[j], sems.at[0, j]).start()

    def spot(col):
        side = ((col >> 2) ^ core) * part
        return (
            pl.ds(pl.multiple_of(side + (col & 3) * size, size), size),
            pl.ds(pl.multiple_of(side + deep + (col & 1) * size, size), size),
            (col >> 1) & 1,
        )

    dists = own.shape[0]
    for j in range(n):
        away, dist = where[j]
        for k in range(most):
            table[j, k] = jnp.where(away == 0, own_table[dist, k], other_table[dist, k])
        table[j, most] = jnp.where(away == 0, own_table[dists, dist], other_table[dists, dist])
    for j in range(n):
        count = table[j, most]
        if not near:
            pltpu.make_async_copy(sources[j], panels[j], sems.at[1, j]).wait()
        if first and j == 0:
            for b in range(blocks):
                weight = jnp.transpose(jnp.broadcast_to(start[b : b + 1, :], (size, LANES)))
                tile, pack, _ = spot(b)
                lanes = (b >> 1) & 1
                acc[0, b] = weight * panels[0][tile, :].astype(F32)
                acc[1 + lanes, b] = weight * panels[0][pack, :].astype(F32)
                acc[2 - lanes, b] = jnp.zeros((size, LANES), F32)
        pltpu.make_async_copy(own.at[0], abuf.at[j], sems.at[0, j]).wait()

        def step(g, carry):
            found = []
            for i in range(UNROLL):
                k = g * UNROLL + i
                entry = table[j, jnp.minimum(k, most - 1)]
                tile, pack, lanes = spot((entry >> 3) & 7)
                row = jnp.where(k < count, entry & 7, blocks)
                right = jnp.concatenate([panels[j][tile, :], panels[j][pack, :]], axis=1)
                product = jnp.dot(abuf[j, entry >> 6], right, preferred_element_type=F32)
                found.append((row, lanes, product))
            for row, lanes, product in found:
                acc[0, row] += product[:, :LANES]
                acc[1 + lanes, row] += product[:, LANES:]
            return carry

        lax.fori_loop(0, (count + UNROLL - 1) // UNROLL, step, 0)
    if last:
        rows = blocks * size
        lane = lax.broadcasted_iota(I32, (size, LANES), 1)
        valid = (lane < LANES // 2) == (core == 0)
        for b in range(blocks):
            out[b * size : (b + 1) * size, :] = acc[0, b].astype(BF16)
            joined = acc[1, b] + pltpu.roll(acc[2, b], LANES // 2, 1)
            turned = pltpu.roll(joined, LANES // 2, 1)
            both = jnp.where(core == 0, joined, turned)
            out[rows + b * size : rows + (b + 1) * size, :] = jnp.where(valid, both, 0.0).astype(BF16)


def gather_call(kinds, near, tables, start, own, other, panels):
    n = len(kinds)
    if near:
        panels = [in_vmem(panel) for panel in panels]
    first, last = kinds[0] == (0, 0, 0), kinds[-1] == (1, 1, 3)
    most, size = own.shape[1], own.shape[2]
    rows = panels[0].shape[0] * 2 // 3
    sums = pltpu.VMEM((3, rows // size + 1, size, LANES), F32)
    outs = (sums, pltpu.VMEM((2 * rows, LANES), BF16)) if last else (sums,)
    start = start if first else in_vmem(start)
    return pl.pallas_call(
        functools.partial(gather_kernel, kinds, near),
        out_shape=outs,
        in_specs=[SMEM_SPEC, SMEM_SPEC, VMEM_SPEC, HBM_SPEC, HBM_SPEC]
        + [VMEM_SPEC if near else HBM_SPEC] * n,
        out_specs=(VMEM_SPEC,) * len(outs),
        input_output_aliases={} if first else {2: 0},
        scratch_shapes=[
            pltpu.VMEM((n, most, size, size), BF16),
            pltpu.SMEM((n, most + 1), I32),
            pltpu.SemaphoreType.DMA((2, n)),
        ]
        + ([] if near else [pltpu.VMEM((n,) + panels[0].shape, BF16)]),
        compiler_params=pltpu.CompilerParams(vmem_limit_bytes=16 << 20),
        cost_estimate=pl.CostEstimate(flops=n * FLOPS, bytes_accessed=n * 800000, transcendentals=0),
    )(*tables, start, own, other, *panels)


def dense_kernel(mine, theirs, w_first, b_first, w_second, *rest):
    outs, (one, two) = rest[:4], rest[4:]
    core = lax.axis_index("rep")
    side = one.shape[1]
    ours = pl.ds(pl.multiple_of(core * side, side), side)
    rows = mine.shape[0] // 2
    agg = jnp.where(core == 0, mine[:rows, :], theirs[:rows, :])
    upper = jnp.where(core == 0, theirs[:rows, :], mine[:rows, :])
    back = jnp.concatenate([mine[rows:, :] + theirs[rows:, :], upper], axis=1)
    pre = jnp.dot(agg, w_first[:, ours], preferred_element_type=F32) + b_first[:, ours]
    squashed = 1.0 / (1.0 + jnp.exp(-pre))
    hidden = (pre * squashed).astype(BF16)
    d_hidden = lax.dot_general(
        back, w_second[ours, :], (((1,), (1,)), ((), ())), preferred_element_type=F32
    )
    grad_pre = (d_hidden * squashed * (1.0 + pre * (1.0 - squashed))).astype(BF16)
    over_rows = (((0,), (0,)), ((), ()))
    two[...] = lax.dot_general(hidden, back, over_rows, preferred_element_type=F32)
    one[...] = lax.dot_general(agg, grad_pre, over_rows, preferred_element_type=F32)
    bias_row = jnp.sum(grad_pre.astype(F32), axis=0, keepdims=True)
    quarter = one.shape[0] // 4
    corner = lax.axis_index("blk") & 3
    for k in range(4):
        span = pl.ds(pl.multiple_of((k ^ corner) * quarter, quarter), quarter)
        outs[k][0:quarter, :] = one[span, :]
        outs[k][quarter : 2 * quarter, :] = two[span, :LANES]
        outs[k][2 * quarter : 3 * quarter, :] = two[span, LANES:]
        outs[k][3 * quarter :, :] = jnp.broadcast_to(bias_row, (8, LANES))


def spread_kernel(*refs):
    pieces, (one, bias, two) = refs[:8], refs[8:]
    core, corner = lax.axis_index("rep"), lax.axis_index("blk") & 3
    quarter = one.shape[0] // 4
    for k in range(4):
        rows = pl.ds(pl.multiple_of((k ^ corner) * quarter, quarter), quarter)
        below = pl.ds(pl.multiple_of(4 * quarter + (k ^ corner) * quarter, quarter), quarter)
        mine, theirs = pieces[k], pieces[4 + k]
        low = jnp.where(core == 0, mine[...], theirs[...])
        high = jnp.where(core == 0, theirs[...], mine[...])
        one[rows, :LANES] = low[:quarter, :]
        one[rows, LANES:] = high[:quarter, :]
        two[rows, :LANES] = low[quarter : 2 * quarter, :]
        two[rows, LANES:] = low[2 * quarter : 3 * quarter, :]
        two[below, :LANES] = high[quarter : 2 * quarter, :]
        two[below, LANES:] = high[2 * quarter : 3 * quarter, :]
        if k == 0:
            bias[:, :LANES] = low[3 * quarter : 3 * quarter + 1, :]
            bias[:, LANES:] = high[3 * quarter : 3 * quarter + 1, :]


def mesh_shards(
    features,
    cotangent,
    self_weight,
    w_first,
    b_first,
    w_second,
    block_row,
    block_col,
    block_slot,
    block_count,
    block_values,
):
    p = lax.axis_index("blk")
    half = features.shape[0]
    rows = 2 * half
    size = block_values.shape[3]
    blocks = rows // size
    hid = w_first.shape[1]

    give = pack_call(True, 3 * half // 2, features, cotangent)
    got = to_sibling(give)
    panel = pack_call(False, 3 * half, features, cotangent)
    panel = lax.dynamic_update_slice(panel, got, (3 * half // 2, 0))

    own = in_hbm(block_values[0])
    held, panel = lax.optimization_barrier((own, panel))
    other = in_hbm(to_sibling(held))
    own_table = pl.pallas_call(
        table_kernel,
        out_shape=jax.ShapeDtypeStruct((2 * block_row.shape[1], LANES), I32),
        in_specs=[VMEM_SPEC] * 4 + [HBM_SPEC],
        out_specs=VMEM_SPEC,
    )(block_row[0], block_col[0], block_slot[0], block_count, panel)
    tables = (own_table, to_sibling(own_table))
    later = lax.optimization_barrier((panel, own_table))[0]
    weights = self_weight.reshape(blocks, size)

    middle = (p // 4 == 1) | (p // 4 == 2)

    def named(name, move, value, *after):
        if after:
            value = lax.optimization_barrier((value,) + after)[0]
        with jax.named_scope(name):
            return move(value)

    def products(name, start, work, near=False):
        kinds = tuple(kind for kind, _ in work)
        with jax.named_scope(name):
            return gather_call(kinds, near, tables, start, own, other, [panel for _, panel in work])

    slot_a = named("TP1", z_pairs, panel)
    one_o = named("TuO", first_way, panel)
    two_o = named("TvO", second_way, panel)
    near = named("TP2", z_middle, later)
    both_o = named("TvuO", second_way, one_o)
    far = named("TP3b", z_middle, slot_a, one_o)
    one_a = named("TuA", first_way, slot_a, two_o)
    slot_b = jnp.where(middle, near, named("TP3a", z_outward, near, slot_a))
    two_a = named("TvA", second_way, slot_a, one_a)
    (first_acc,) = products("TK0", weights, [((0, 0, 0), panel), ((1, 0, 0), one_o), ((0, 1, 0), two_o)])
    one_b = named("TuB", first_way, slot_b, one_a, other)
    two_b = named("TvB", second_way, slot_b, one_a, two_a, first_acc)
    (acc,) = products("TK1", first_acc, [((1, 1, 0), both_o), ((0, 0, 1), slot_a), ((1, 0, 1), one_a), ((1, 0, 2), one_b)])
    slot_c = named("TP4", z_outward, far, both_o, one_a)
    slot_c = jnp.where(middle, lax.optimization_barrier((far, first_acc))[0], slot_c)
    both_b = named("TvuB", second_way, one_b)
    both_a = named("TvuA", z_pairs, both_o, slot_c)
    one_c = named("TuC", first_way, slot_c)
    two_c = named("TvC", second_way, slot_c, two_b, acc)
    (acc,) = products("TK2", acc, [((0, 1, 1), two_a), ((0, 0, 2), slot_b), ((0, 1, 2), two_b)])
    both_c = named("TvuC", second_way, one_c, acc)
    (acc,) = products("TK3", acc, [((1, 1, 2), both_b), ((0, 0, 3), slot_c), ((1, 0, 3), one_c), ((0, 1, 3), two_c)], True)
    _, summed = products("TK4", acc, [((1, 1, 1), both_a), ((1, 1, 3), both_c)], True)
    from_sibling = in_vmem(to_sibling(summed))

    side = hid // 2
    pieces = pl.pallas_call(
        dense_kernel,
        out_shape=(pltpu.VMEM((3 * side // 4 + 8, LANES), F32),) * 4,
        in_specs=[VMEM_SPEC] * 5,
        out_specs=(VMEM_SPEC,) * 4,
        scratch_shapes=[pltpu.VMEM((side, side), F32), pltpu.VMEM((side, hid), F32)],
    )(in_vmem(summed), from_sibling, w_first, b_first[None, :], w_second)

    def in_plane(value, k):
        return send(value, lambda p, r: (p ^ k, r))

    got = [in_plane(pieces[k], k) for k in (1, 2, 3)]
    total = (pieces[0] + got[0]) + (got[1] + got[2])
    across = [in_plane(total, 4 * k) for k in (1, 2, 3)]
    total = (total + across[0]) + (across[1] + across[2])
    full = [total] + [in_plane(total, k) for k in (1, 2, 3)]
    back = [in_vmem(to_sibling(value)) for value in full]
    full = [in_vmem(value) for value in full]
    grad_w1, grad_b1, grad_w2 = pl.pallas_call(
        spread_kernel,
        out_shape=(
            jax.ShapeDtypeStruct((side, hid), F32),
            jax.ShapeDtypeStruct((1, hid), F32),
            jax.ShapeDtypeStruct((hid, hid), F32),
        ),
        in_specs=[VMEM_SPEC] * 8,
        out_specs=(VMEM_SPEC,) * 3,
    )(*full, *back)
    return (grad_w1, grad_b1.reshape(hid), grad_w2)


def solution(mesh):
    placed = (
        P(("blk", "rep"), None),
        P(("blk", "rep"), None),
        P("blk"),
        P(),
        P(),
        P(),
        P("blk", "rep", None),
        P("blk", "rep", None),
        P("blk", "rep", None),
        P("blk", "rep"),
        P("blk", "rep", None, None, None),
    )
    fits = mesh.shape["blk"] == 16 and mesh.shape["rep"] == 2
    return jax.shard_map(
        mesh_shards if fits else walk_shards, mesh=mesh, in_specs=placed, out_specs=(P(), P(), P()), check_vma=False
    )
```

```python
import functools

import jax
import jax.numpy as jnp
from jax import lax
from jax.experimental import pallas as pl
from jax.experimental.pallas import tpu as pltpu
from jax.sharding import PartitionSpec as P


def passed_along(value, axis, steps):
    count = lax.axis_size(axis)
    pairs = [(source, (source + steps) % count) for source in range(count)]
    return lax.ppermute(value, axis, pairs)


def contribute(running, panel_now, position, tables):
    local_rows, local_cols, live_mask, ordered = tables
    row_ids = lax.dynamic_index_in_dim(local_rows, position, 0, keepdims=False)
    col_ids = lax.dynamic_index_in_dim(local_cols, position, 0, keepdims=False)
    live_now = lax.dynamic_index_in_dim(live_mask, position, 0, keepdims=False)
    blocks = lax.dynamic_index_in_dim(ordered, position, 0, keepdims=False)
    picked = jnp.take(panel_now, col_ids, axis=0)
    product = jnp.einsum("mab,mbf->maf", blocks, picked, preferred_element_type=jnp.float32)
    row_range = jnp.arange(panel_now.shape[0], dtype=jnp.int32)
    onehot = jnp.where(row_ids[None, :] == row_range[:, None], live_now[None, :], 0.0)
    return running + jnp.einsum("rm,maf->raf", onehot, product, precision=lax.Precision.HIGHEST)


def walk_shards(
    features,
    cotangent,
    self_weight,
    w_first,
    b_first,
    w_second,
    block_row,
    block_col,
    block_slot,
    block_count,
    block_values,
):
    rep_index = lax.axis_index("rep")
    bit_count = lax.axis_size("rep").bit_length() - 1
    cycle_steps = block_values.shape[1]
    most_blocks = block_values.shape[2]
    block_size = block_values.shape[3]
    in_width = features.shape[1]
    hid_width = cotangent.shape[1]
    x_full, g_full = (
        lax.all_gather(features, "rep", axis=0, tiled=True),
        lax.all_gather(cotangent, "rep", axis=0, tiled=True),
    )
    rows_total = x_full.shape[0]
    row_blocks = rows_total // block_size
    live_mask = jnp.where(
        jnp.arange(most_blocks, dtype=jnp.int32)[None, :] < block_count[0][:, None], 1.0, 0.0
    ).astype(jnp.float32)
    ordered = jnp.take_along_axis(block_values[0], block_slot[0][:, :, None, None], axis=1)
    tables = (block_row[0] % row_blocks, block_col[0] % row_blocks, live_mask, ordered)
    x_panel = x_full.reshape(row_blocks, block_size, in_width)
    g_panel = g_full.reshape(row_blocks, block_size, hid_width)
    moving_x = x_panel
    for bit_level in range(bit_count):
        shifted_x = passed_along(moving_x, "blk", cycle_steps << bit_level)
        moving_x = jnp.where(rep_index >> bit_level & 1 == 1, shifted_x, moving_x)
    first_x = contribute(
        jnp.zeros((row_blocks, block_size, in_width), jnp.float32), moving_x, 0, tables
    )

    def walk_x(position, loop_state):
        held_panel, running = loop_state
        held_panel = passed_along(held_panel, "blk", 1)
        return (held_panel, contribute(running, held_panel, position, tables))

    total_x = lax.fori_loop(1, cycle_steps, walk_x, (moving_x, first_x))[1]
    moving_g = g_panel
    for bit_level in range(bit_count):
        shifted_g = passed_along(moving_g, "blk", cycle_steps << bit_level)
        moving_g = jnp.where(rep_index >> bit_level & 1 == 1, shifted_g, moving_g)
    first_g = contribute(
        jnp.zeros((row_blocks, block_size, hid_width), jnp.float32), moving_g, 0, tables
    )

    def walk_g(position, loop_state):
        held_panel, running = loop_state
        held_panel = passed_along(held_panel, "blk", 1)
        return (held_panel, contribute(running, held_panel, position, tables))

    total_g = lax.fori_loop(1, cycle_steps, walk_g, (moving_g, first_g))[1]
    part_x_all = total_x.reshape(rows_total, in_width)
    part_g_all = total_g.reshape(rows_total, hid_width)
    part_x, part_g = lax.psum((part_x_all, part_g_all), "rep")
    aggregated = (part_x + self_weight[:, None] * x_full.astype(jnp.float32)).astype(jnp.bfloat16)
    pre_act = jnp.dot(aggregated, w_first, preferred_element_type=jnp.float32) + b_first
    hidden = jax.nn.silu(pre_act).astype(jnp.bfloat16)
    back_agg = (part_g + self_weight[:, None] * g_full.astype(jnp.float32)).astype(jnp.bfloat16)
    grad_w2 = jnp.einsum("nh,nk->hk", hidden, back_agg, preferred_element_type=jnp.float32)
    squashed = jax.nn.sigmoid(pre_act)
    d_hidden = jnp.einsum("nk,hk->nh", back_agg, w_second, preferred_element_type=jnp.float32)
    grad_pre = (d_hidden * squashed * (1.0 + pre_act * (1.0 - squashed))).astype(jnp.bfloat16)
    grad_w1 = jnp.einsum("nf,nh->fh", aggregated, grad_pre, preferred_element_type=jnp.float32)
    grad_b1 = jnp.sum(grad_pre.astype(jnp.float32), axis=0)
    grad_w1, grad_b1, grad_w2 = lax.psum((grad_w1, grad_b1, grad_w2), "blk")
    return (grad_w1, grad_b1, grad_w2)

BF16, F32, I32 = jnp.bfloat16, jnp.float32, jnp.int32
LANES = 128
VMEM_SPEC = pl.BlockSpec(memory_space=pltpu.VMEM)
SMEM_SPEC = pl.BlockSpec(memory_space=pltpu.SMEM)
HBM_SPEC = pl.BlockSpec(memory_space=pltpu.HBM)


def send(value, target):
    pairs = []
    for p in range(16):
        for r in range(2):
            to = target(p, r)
            if to is not None:
                pairs.append((p * 2 + r, to[0] * 2 + to[1]))
    return lax.ppermute(value, ("blk", "rep"), pairs)


def in_hbm(value):
    return pltpu.with_memory_space_constraint(value, pltpu.HBM)


def in_vmem(value):
    return pltpu.with_memory_space_constraint(value, pltpu.VMEM)


def to_sibling(value):
    return send(value, lambda p, r: (p, 1 - r))


def first_way(value):
    return send(value, lambda p, r: (p ^ (1 + r), r))


def second_way(value):
    return send(value, lambda p, r: (p ^ (2 - r), r))


def z_pairs(value):
    return send(value, lambda p, r: (p ^ 4, r))


def z_middle(value):
    return send(value, lambda p, r: (p ^ 12, r) if p // 4 in (1, 2) else None)


def z_outward(value):
    return send(value, lambda p, r: (p ^ 4, r) if p // 4 in (1, 2) else None)


def pack_kernel(away, feat, cot, out):
    core = lax.axis_index("rep")
    core = 1 - core if away else core
    half, deep = feat.shape[0], feat.shape[0] // 2
    lane = lax.broadcasted_iota(I32, (deep, LANES), 1)
    above, below = cot[:deep, :LANES], cot[deep:, :LANES]

    def turned(value):
        return pltpu.roll(value.astype(F32), LANES // 2, 1).astype(BF16)

    @pl.when(core == 0)
    def _():
        out[:half, :] = feat[...]
        out[half : half + deep, :] = jnp.where(lane < LANES // 2, above, turned(below))

    @pl.when(core == 1)
    def _():
        out[:half, :] = cot[:, LANES:]
        out[half : half + deep, :] = jnp.where(lane < LANES // 2, turned(above), below)


def pack_call(away, rows, features, cotangent):
    return pl.pallas_call(
        functools.partial(pack_kernel, away),
        out_shape=pltpu.VMEM((rows, LANES), BF16),
        in_specs=[VMEM_SPEC] * 2,
        out_specs=VMEM_SPEC,
    )(features, cotangent)


def table_kernel(row, col, slot, count, after, table):
    dists, most = row.shape
    table[:dists, :most] = (row[...] & 7) + 8 * (col[...] & 7) + 64 * slot[...]
    table[dists : dists + 1, :dists] = count[...]


def entry_of(p, core, kind):
    step_one, step_two, slot = kind
    z, w = p >> 2, p & 3
    if step_one:
        w = w ^ (1 + core)
    if step_two:
        w = w ^ (2 - core)
    upper = z >> 1
    z = (z, z ^ 1, 2 - upper, 3 - 3 * upper)[slot]
    d = (p - (z * 4 + w)) & 15
    return (d >> 3) ^ core, d & 7


UNROLL = 6
FLOPS = 300000000


def gather_kernel(kinds, near, own_table, other_table, start, own, other, *rest):
    n = len(kinds)
    first, last = kinds[0] == (0, 0, 0), kinds[-1] == (1, 1, 3)
    sources, acc, rest = rest[:n], rest[n], rest[n + 1 :]
    if last:
        out, rest = rest[0], rest[1:]
    abuf, table, sems = rest[:3]
    panels = sources if near else [rest[3].at[j] for j in range(n)]
    most = abuf.shape[1]
    blocks = acc.shape[1] - 1
    size = acc.shape[2]
    part = sources[0].shape[0] // 2
    deep = part * 2 // 3
    core = lax.axis_index("rep")
    where = [entry_of(lax.axis_index("blk"), core, kind) for kind in kinds]
    for j in range(n):
        away, dist = where[j]
        if not near:
            pltpu.make_async_copy(sources[j], panels[j], sems.at[1, j]).start()

        @pl.when(away == 0)
        def _():
            pltpu.make_async_copy(own.at[dist], abuf.at[j], sems.at[0, j]).start()

        @pl.when(away != 0)
        def _():
            pltpu.make_async_copy(other.at[dist], abuf.at[j], sems.at[0, j]).start()

    def spot(col):
        side = ((col >> 2) ^ core) * part
        return (
            pl.ds(pl.multiple_of(side + (col & 3) * size, size), size),
            pl.ds(pl.multiple_of(side + deep + (col & 1) * size, size), size),
            (col >> 1) & 1,
        )

    dists = own.shape[0]
    for j in range(n):
        away, dist = where[j]
        for k in range(most):
            table[j, k] = jnp.where(away == 0, own_table[dist, k], other_table[dist, k])
        table[j, most] = jnp.where(away == 0, own_table[dists, dist], other_table[dists, dist])
    for j in range(n):
        count = table[j, most]
        if not near:
            pltpu.make_async_copy(sources[j], panels[j], sems.at[1, j]).wait()
        if first and j == 0:
            for b in range(blocks):
                weight = jnp.transpose(jnp.broadcast_to(start[b : b + 1, :], (size, LANES)))
                tile, pack, _ = spot(b)
                lanes = (b >> 1) & 1
                acc[0, b] = weight * panels[0][tile, :].astype(F32)
                acc[1 + lanes, b] = weight * panels[0][pack, :].astype(F32)
                acc[2 - lanes, b] = jnp.zeros((size, LANES), F32)
        pltpu.make_async_copy(own.at[0], abuf.at[j], sems.at[0, j]).wait()

        def step(g, carry):
            found = []
            for i in range(UNROLL):
                k = g * UNROLL + i
                entry = table[j, jnp.minimum(k, most - 1)]
                tile, pack, lanes = spot((entry >> 3) & 7)
                row = jnp.where(k < count, entry & 7, blocks)
                right = jnp.concatenate([panels[j][tile, :], panels[j][pack, :]], axis=1)
                product = jnp.dot(abuf[j, entry >> 6], right, preferred_element_type=F32)
                found.append((row, lanes, product))
            for row, lanes, product in found:
                acc[0, row] += product[:, :LANES]
                acc[1 + lanes, row] += product[:, LANES:]
            return carry

        lax.fori_loop(0, (count + UNROLL - 1) // UNROLL, step, 0)
    if last:
        rows = blocks * size
        lane = lax.broadcasted_iota(I32, (size, LANES), 1)
        valid = (lane < LANES // 2) == (core == 0)
        for b in range(blocks):
            out[b * size : (b + 1) * size, :] = acc[0, b].astype(BF16)
            joined = acc[1, b] + pltpu.roll(acc[2, b], LANES // 2, 1)
            turned = pltpu.roll(joined, LANES // 2, 1)
            both = jnp.where(core == 0, joined, turned)
            out[rows + b * size : rows + (b + 1) * size, :] = jnp.where(valid, both, 0.0).astype(BF16)


def gather_call(kinds, near, tables, start, own, other, panels):
    n = len(kinds)
    if near:
        panels = [in_vmem(panel) for panel in panels]
    first, last = kinds[0] == (0, 0, 0), kinds[-1] == (1, 1, 3)
    most, size = own.shape[1], own.shape[2]
    rows = panels[0].shape[0] * 2 // 3
    sums = pltpu.VMEM((3, rows // size + 1, size, LANES), F32)
    outs = (sums, pltpu.VMEM((2 * rows, LANES), BF16)) if last else (sums,)
    start = start if first else in_vmem(start)
    return pl.pallas_call(
        functools.partial(gather_kernel, kinds, near),
        out_shape=outs,
        in_specs=[SMEM_SPEC, SMEM_SPEC, VMEM_SPEC, HBM_SPEC, HBM_SPEC]
        + [VMEM_SPEC if near else HBM_SPEC] * n,
        out_specs=(VMEM_SPEC,) * len(outs),
        input_output_aliases={} if first else {2: 0},
        scratch_shapes=[
            pltpu.VMEM((n, most, size, size), BF16),
            pltpu.SMEM((n, most + 1), I32),
            pltpu.SemaphoreType.DMA((2, n)),
        ]
        + ([] if near else [pltpu.VMEM((n,) + panels[0].shape, BF16)]),
        compiler_params=pltpu.CompilerParams(vmem_limit_bytes=16 << 20),
        cost_estimate=pl.CostEstimate(flops=n * FLOPS, bytes_accessed=n * 800000, transcendentals=0),
    )(*tables, start, own, other, *panels)


def dense_kernel(mine, theirs, w_first, b_first, w_second, *rest):
    outs, (one, two) = rest[:4], rest[4:]
    core = lax.axis_index("rep")
    side = one.shape[1]
    ours = pl.ds(pl.multiple_of(core * side, side), side)
    rows = mine.shape[0] // 2
    agg = jnp.where(core == 0, mine[:rows, :], theirs[:rows, :])
    upper = jnp.where(core == 0, theirs[:rows, :], mine[:rows, :])
    back = jnp.concatenate([mine[rows:, :] + theirs[rows:, :], upper], axis=1)
    pre = jnp.dot(agg, w_first[:, ours], preferred_element_type=F32) + b_first[:, ours]
    squashed = 1.0 / (1.0 + jnp.exp(-pre))
    hidden = (pre * squashed).astype(BF16)
    d_hidden = lax.dot_general(
        back, w_second[ours, :], (((1,), (1,)), ((), ())), preferred_element_type=F32
    )
    grad_pre = (d_hidden * squashed * (1.0 + pre * (1.0 - squashed))).astype(BF16)
    over_rows = (((0,), (0,)), ((), ()))
    two[...] = lax.dot_general(hidden, back, over_rows, preferred_element_type=F32)
    one[...] = lax.dot_general(agg, grad_pre, over_rows, preferred_element_type=F32)
    bias_row = jnp.sum(grad_pre.astype(F32), axis=0, keepdims=True)
    quarter = one.shape[0] // 4
    corner = lax.axis_index("blk") & 3
    for k in range(4):
        span = pl.ds(pl.multiple_of((k ^ corner) * quarter, quarter), quarter)
        outs[k][0:quarter, :] = one[span, :]
        outs[k][quarter : 2 * quarter, :] = two[span, :LANES]
        outs[k][2 * quarter : 3 * quarter, :] = two[span, LANES:]
        outs[k][3 * quarter :, :] = jnp.broadcast_to(bias_row, (8, LANES))


def spread_kernel(*refs):
    pieces, (one, bias, two) = refs[:8], refs[8:]
    core, corner = lax.axis_index("rep"), lax.axis_index("blk") & 3
    quarter = one.shape[0] // 4
    for k in range(4):
        rows = pl.ds(pl.multiple_of((k ^ corner) * quarter, quarter), quarter)
        below = pl.ds(pl.multiple_of(4 * quarter + (k ^ corner) * quarter, quarter), quarter)
        mine, theirs = pieces[k], pieces[4 + k]
        low = jnp.where(core == 0, mine[...], theirs[...])
        high = jnp.where(core == 0, theirs[...], mine[...])
        one[rows, :LANES] = low[:quarter, :]
        one[rows, LANES:] = high[:quarter, :]
        two[rows, :LANES] = low[quarter : 2 * quarter, :]
        two[rows, LANES:] = low[2 * quarter : 3 * quarter, :]
        two[below, :LANES] = high[quarter : 2 * quarter, :]
        two[below, LANES:] = high[2 * quarter : 3 * quarter, :]
        if k == 0:
            bias[:, :LANES] = low[3 * quarter : 3 * quarter + 1, :]
            bias[:, LANES:] = high[3 * quarter : 3 * quarter + 1, :]


def mesh_shards(
    features,
    cotangent,
    self_weight,
    w_first,
    b_first,
    w_second,
    block_row,
    block_col,
    block_slot,
    block_count,
    block_values,
):
    p = lax.axis_index("blk")
    half = features.shape[0]
    rows = 2 * half
    size = block_values.shape[3]
    blocks = rows // size
    hid = w_first.shape[1]

    give = pack_call(True, 3 * half // 2, features, cotangent)
    got = to_sibling(give)
    panel = pack_call(False, 3 * half, features, cotangent)
    panel = lax.dynamic_update_slice(panel, got, (3 * half // 2, 0))

    own = in_hbm(block_values[0])
    held, panel = lax.optimization_barrier((own, panel))
    other = in_hbm(to_sibling(held))
    own_table = pl.pallas_call(
        table_kernel,
        out_shape=jax.ShapeDtypeStruct((2 * block_row.shape[1], LANES), I32),
        in_specs=[VMEM_SPEC] * 4 + [HBM_SPEC],
        out_specs=VMEM_SPEC,
    )(block_row[0], block_col[0], block_slot[0], block_count, panel)
    tables = (own_table, to_sibling(own_table))
    later = lax.optimization_barrier((panel, own_table))[0]
    weights = self_weight.reshape(blocks, size)

    middle = (p // 4 == 1) | (p // 4 == 2)

    def named(name, move, value, *after):
        if after:
            value = lax.optimization_barrier((value,) + after)[0]
        with jax.named_scope(name):
            return move(value)

    def products(name, start, work, near=False):
        kinds = tuple(kind for kind, _ in work)
        with jax.named_scope(name):
            return gather_call(kinds, near, tables, start, own, other, [panel for _, panel in work])

    slot_a = named("TP1", z_pairs, panel)
    one_o = named("TuO", first_way, panel)
    two_o = named("TvO", second_way, panel)
    near = named("TP2", z_middle, panel)
    both_o = named("TvuO", second_way, one_o)
    far = named("TP3b", z_middle, slot_a, one_o)
    one_a = named("TuA", first_way, slot_a, two_o)
    slot_b = jnp.where(middle, near, named("TP3a", z_outward, near, slot_a))
    two_a = named("TvA", second_way, slot_a, one_a)
    (first_acc,) = products("TK0", weights, [((0, 0, 0), panel), ((1, 0, 0), one_o), ((0, 1, 0), two_o)])
    one_b = named("TuB", first_way, slot_b, one_a, other)
    two_b = named("TvB", second_way, slot_b, one_a, two_a, first_acc)
    (acc,) = products("TK1", first_acc, [((1, 1, 0), both_o), ((0, 0, 1), slot_a), ((1, 0, 1), one_a), ((1, 0, 2), one_b)])
    slot_c = named("TP4", z_outward, far, both_o, one_a)
    slot_c = jnp.where(middle, lax.optimization_barrier((far, first_acc))[0], slot_c)
    both_b = named("TvuB", second_way, one_b)
    both_a = named("TvuA", z_pairs, both_o, slot_c)
    one_c = named("TuC", first_way, slot_c)
    two_c = named("TvC", second_way, slot_c, two_b, acc)
    (acc,) = products("TK2", acc, [((0, 1, 1), two_a), ((0, 0, 2), slot_b), ((0, 1, 2), two_b)])
    both_c = named("TvuC", second_way, one_c, acc)
    (acc,) = products("TK3", acc, [((1, 1, 2), both_b), ((0, 0, 3), slot_c), ((1, 0, 3), one_c), ((0, 1, 3), two_c)], True)
    _, summed = products("TK4", acc, [((1, 1, 1), both_a), ((1, 1, 3), both_c)], True)
    from_sibling = in_vmem(to_sibling(summed))

    side = hid // 2
    pieces = pl.pallas_call(
        dense_kernel,
        out_shape=(pltpu.VMEM((3 * side // 4 + 8, LANES), F32),) * 4,
        in_specs=[VMEM_SPEC] * 5,
        out_specs=(VMEM_SPEC,) * 4,
        scratch_shapes=[pltpu.VMEM((side, side), F32), pltpu.VMEM((side, hid), F32)],
    )(in_vmem(summed), from_sibling, w_first, b_first[None, :], w_second)

    def in_plane(value, k):
        return send(value, lambda p, r: (p ^ k, r))

    got = [in_plane(pieces[k], k) for k in (1, 2, 3)]
    total = (pieces[0] + got[0]) + (got[1] + got[2])
    across = [in_plane(total, 4 * k) for k in (1, 2, 3)]
    total = (total + across[0]) + (across[1] + across[2])
    full = [total] + [in_plane(total, k) for k in (1, 2, 3)]
    back = [in_vmem(to_sibling(value)) for value in full]
    full = [in_vmem(value) for value in full]
    grad_w1, grad_b1, grad_w2 = pl.pallas_call(
        spread_kernel,
        out_shape=(
            jax.ShapeDtypeStruct((side, hid), F32),
            jax.ShapeDtypeStruct((1, hid), F32),
            jax.ShapeDtypeStruct((hid, hid), F32),
        ),
        in_specs=[VMEM_SPEC] * 8,
        out_specs=(VMEM_SPEC,) * 3,
    )(*full, *back)
    return (grad_w1, grad_b1.reshape(hid), grad_w2)


def solution(mesh):
    placed = (
        P(("blk", "rep"), None),
        P(("blk", "rep"), None),
        P("blk"),
        P(),
        P(),
        P(),
        P("blk", "rep", None),
        P("blk", "rep", None),
        P("blk", "rep", None),
        P("blk", "rep"),
        P("blk", "rep", None, None, None),
    )
    fits = mesh.shape["blk"] == 16 and mesh.shape["rep"] == 2
    return jax.shard_map(
        mesh_shards if fits else walk_shards, mesh=mesh, in_specs=placed, out_specs=(P(), P(), P()), check_vma=False
    )
```
